32 devices in a mesh: by: 4 (over y, x), bx: 8 (over z, core).
Axes of the slice: x: 2, y: 2, z: 4, core: 2. Of those that a mesh axis runs over, the one named last changes fastest.
Arguments:
- tracers: float32 [2, 8, 384, 1024], P(None, None, 'by', 'bx'), may hold values from -6 to 6
- velocity: float32 [2, 8, 384, 1024], P(None, None, 'by', 'bx'), may hold values from -0.4 to 0.4
- diffusivity: float32 [8, 384, 1024], P(None, 'by', 'bx'), may hold values from 0.02 to 0.2
- kmt: int32 [384, 1024], P('by', 'bx'), may hold values from 0 to 8
- forcing: float32 [384, 1024], P('by', 'bx'), may hold values from -6 to 6
- free_surface: float32 [384, 1024], P('by', 'bx'), may hold values from 0.25 to 2
Outputs:
- new_tracers: float32 [2, 8, 384, 1024], P(None, None, 'by', 'bx')
- surface: float32 [384, 1024], P('by', 'bx')
- residual: float32 [384, 1024], P('by', 'bx')
The draws below stay inside these ranges and needn't reach their ends.
All inputs are finite; a program needn't handle non-finite values.
Results may differ from the reference program's by a relative error of at most 0.0003.
Values sent between devices are 32-bit elements; how exact they have to be, the bound alone decides.
No kernel may reach another device: no remote copies, remote signals or barrier semaphores. Data moves between devices by JAX's collectives and lax.ppermute only.
A program may use at most 64 MiB of HBM per device.

```python
import math
import jax
import jax.numpy as jnp

LEV = 8
TRACERS = 2
ITERS = 4
NY = 384
NX = 1024


def plant(array, key, smallest, largest):
    longest = array.shape.index(max(array.shape))
    spots = []
    for shift in (0, 1):
        where = [jax.random.randint(jax.random.fold_in(key, axis), (), 0, length) for axis, length in enumerate(array.shape)]
        where[longest] = (where[longest] + shift) % array.shape[longest]
        spots.append(tuple(where))
    return array.at[spots[0]].set(smallest).at[spots[1]].set(largest)


def level_of(own_key, extent, cuts, low, largest):
    gain, own = 1.0, jax.random.fold_in(own_key, 6)
    for position, blocks in cuts:
        heights = jnp.exp(jax.random.uniform(jax.random.fold_in(own, position), (blocks,), jnp.float32, low / len(cuts), largest / len(cuts)))
        gain = gain * jnp.repeat(heights, extent[position] // blocks).reshape([-1 if axis == position else 1 for axis in range(len(extent))])
    return gain


def gaussian(rng, shape, scale, reach, cuts=(), held_as=jnp.bfloat16):
    array = scale * jax.random.normal(rng, shape, jnp.float32)
    if cuts:
        array = array * level_of(rng, shape, cuts, -0.22, 0.18)
    return jnp.clip(array, -reach, reach).astype(held_as)


def setup_inputs(seed: int = 0) -> dict:
    streams_of = jax.random.split(jax.random.key(seed), 7)
    tracers = gaussian(streams_of[0], (TRACERS, LEV, NY, NX), 1.0, 6.0, ((2, 4), (3, 8)), jnp.float32)
    velocity = jnp.clip(jax.random.uniform(streams_of[1], (2, LEV, NY, NX), jnp.float32, -0.4, 0.4) * level_of(streams_of[1], (2, LEV, NY, NX), ((2, 4), (3, 8)), -0.4, 0.0), -0.4, 0.4)
    diffusivity = jnp.clip(jnp.exp(math.log(0.2) - 2.3025851 * jax.random.uniform(streams_of[2], (LEV, NY, NX), jnp.float32) ** level_of(streams_of[2], (LEV, NY, NX), ((1, 4), (2, 8)), -0.2, 0.2)), 0.02, 0.2)
    kmt = plant(jax.random.randint(streams_of[3], (NY, NX), 0, LEV + 1), jax.random.fold_in(streams_of[3], 1), 0, LEV).astype(jnp.int32)
    forcing = gaussian(streams_of[4], (NY, NX), 1.0, 6.0, ((0, 4), (1, 8)), jnp.float32)
    free_surface = jnp.clip(0.25 + 1.75 * jax.random.uniform(streams_of[5], (NY, NX), jnp.float32) ** level_of(streams_of[5], (NY, NX), ((0, 4), (1, 8)), -0.2, 0.2), 0.25, 2.0)
    return dict(tracers=tracers, velocity=velocity, diffusivity=diffusivity, kmt=kmt, forcing=forcing, free_surface=free_surface)


def four_sides(field):
    padded = jnp.pad(field, 1)
    return padded[1:-1, 2:] + padded[1:-1, :-2] + padded[2:, 1:-1] + padded[:-2, 1:-1]


def reference(tracers, velocity, diffusivity, kmt, forcing, free_surface):
    levels = jnp.arange(LEV, dtype=jnp.int32)
    mask = (levels[:, None, None] < kmt[None]).astype(jnp.float32)
    masked = tracers * mask[None]
    padded = jnp.pad(masked, ((0, 0), (0, 0), (1, 1), (1, 1)))
    east = padded[:, :, 1:-1, 2:]
    west = padded[:, :, 1:-1, :-2]
    north = padded[:, :, 2:, 1:-1]
    south = padded[:, :, :-2, 1:-1]
    lap = east + west + north + south - 4.0 * masked
    adv = 0.5 * (velocity[0][None] * (east - west) + velocity[1][None] * (north - south))
    new_tracers = mask[None] * (tracers + diffusivity[None] * lap - adv)
    ocean = (kmt > 0).astype(jnp.float32)
    weight = ocean * (4.0 + free_surface)
    rhs = ocean * (forcing + jnp.sum(new_tracers[0] - new_tracers[1], axis=0) / LEV)

    def operate(field):
        return weight * field - ocean * four_sides(field)

    surface = jnp.zeros_like(rhs)
    residual = rhs
    image = operate(residual)
    norm_now = jnp.sum(residual * residual)
    product = jnp.sum(residual * image)
    alpha = norm_now / product
    direction, along = residual, image
    for step in range(ITERS):
        surface = surface + alpha * direction
        residual = residual - alpha * along
        if step + 1 < ITERS:
            image = operate(residual)
            norm_next = jnp.sum(residual * residual)
            product = jnp.sum(residual * image)
            ratio = norm_next / norm_now
            alpha = norm_next / (product - ratio * norm_next / alpha)
            direction = residual + ratio * direction
            along = image + ratio * along
            norm_now = norm_next
    return new_tracers, surface, residual
```

```python
import functools

import jax
import jax.numpy as jnp
from jax import lax
from jax.experimental import pallas as pl
from jax.experimental.pallas import tpu as pltpu
from jax.sharding import PartitionSpec as P

ITERS = 4
TILE = 8
REACH = 4
CENTER = 5.0
HALFWIDTH = 4.0
LIMIT = 1000.0


def lanes_of(shape):
    return lax.broadcasted_iota(jnp.int32, shape, 1)


def rows_of(shape):
    return lax.broadcasted_iota(jnp.int32, shape, 0)


def roll(value, shift, axis=1):
    size = value.shape[axis]
    shift = shift % size
    return value if shift == 0 else pltpu.roll(value, shift, axis)


def grouped_sum(value, first, last):
    step = first
    while step < last:
        value = value + roll(value, step)
        step *= 2
    return value


def stencil_kernel(tr, ve, di, kmt_ref, fo, fs, new, packed, top, bottom, rhs_out):
    levels = tr.shape[1]
    rows, cols = kmt_ref.shape
    shape = (rows, cols)
    lane, row = lanes_of(shape), rows_of(shape)
    kmt = kmt_ref[...]
    zero = jnp.zeros(shape, jnp.float32)
    total, pack = zero, zero
    for k in range(levels):
        wet = kmt > k
        mixing = jnp.where(wet, di[k], zero)
        across = jnp.where(wet, 0.5 * ve[0, k], zero)
        along = jnp.where(wet, 0.5 * ve[1, k], zero)
        c_east, c_west = mixing - across, mixing + across
        c_north, c_south = mixing - along, mixing + along
        edge = jnp.where(lane == cols - 1, c_east, c_west)
        top[pl.ds(2 * levels + k, 1), :] = c_north[rows - 1 :, :]
        bottom[pl.ds(2 * levels + k, 1), :] = c_south[:1, :]
        c_east = jnp.where(lane == cols - 1, zero, c_east)
        c_west = jnp.where(lane == 0, zero, c_west)
        c_north = jnp.where(row == rows - 1, zero, c_north)
        c_south = jnp.where(row == 0, zero, c_south)
        own = 1.0 - 4.0 * mixing
        pack = jnp.where((lane // 2) == 2 * levels + k, roll(edge, 4 * levels + 2 * k + 1), pack)
        for t in range(2):
            value = jnp.where(wet, tr[t, k], zero)
            moved = (
                value * own
                + c_east * roll(value, -1)
                + c_west * roll(value, 1)
                + c_north * roll(value, -1, 0)
                + c_south * roll(value, 1, 0)
            )
            new[t, k] = moved
            total = total + moved if t == 0 else total - moved
            top[pl.ds(t * levels + k, 1), :] = value[rows - 1 :, :]
            bottom[pl.ds(t * levels + k, 1), :] = value[:1, :]
            pack = jnp.where((lane // 2) == t * levels + k, roll(value, 2 * (t * levels + k) + 1), pack)
    rhs = jnp.where(kmt > 0, fo[...] + total / levels, zero)
    rhs_out[...] = rhs
    base = 6 * levels
    for i, field in enumerate((rhs, kmt.astype(jnp.float32), fs[...])):
        pack = jnp.where((lane // 8) == base // 8 + i, roll(field, base + 8 * i + REACH), pack)
    packed[pl.ds(0, rows), :] = pack
    small = (levels, cols)
    lane_s, row_s = lanes_of(small), rows_of(small)
    corner = jnp.zeros((TILE, cols), jnp.float32)
    row_c = rows_of((TILE, cols))
    for i, ref in enumerate((bottom, top)):
        jump = ref[pl.ds(0, levels), :] - ref[pl.ds(levels, levels), :]
        past = ref[pl.ds(2 * levels, levels), :]
        line = jnp.zeros(small, jnp.float32)
        for start, field in ((0, jump), (8 * levels, past)):
            spread = pltpu.roll(field, (start + REACH) % cols, 1, stride=8, stride_axis=0)
            line = line + jnp.where((lane_s // 8) == start // 8 + row_s, spread, 0.0)
        corner = jnp.where(row_c == i, jnp.sum(line, axis=0, keepdims=True), corner)
    packed[pl.ds(rows, TILE), :] = corner


def sides(even, last, index, got_a, got_b):
    after = jnp.where(even, got_a, got_b)
    before = jnp.where(even, got_b, got_a)
    return jnp.where(index < last, after, 0.0), jnp.where(index > 0, before, 0.0)


def columns_kernel(places, got_a, got_b, packed, top, bottom, kmt, fs, rhs_in, strip_out, rhs_out, send_a, send_b):
    rows, cols = kmt.shape
    levels = top.shape[0] // 3
    east, west = sides(places[0] == 1, places[2], places[1], got_a[...], got_b[...])
    shape = (rows, cols)
    lane = lanes_of(shape)
    mine = packed[pl.ds(0, rows), :]
    e, w = east[:rows], west[:rows]
    beyond = jnp.where(lane % 2 == 0, roll(e, -1), roll(w, 1))
    jump_beyond = roll(beyond, 4 * levels) - roll(beyond, 2 * levels)
    jump_mine = roll(mine, 4 * levels) - roll(mine, 2 * levels)
    here = (lane >= 4 * levels) & (lane < 6 * levels)
    inward = jnp.where(here, mine * jump_beyond, 0.0)
    outward = jnp.where(here, beyond * jump_mine, 0.0)
    both = inward + roll(outward, 2 * levels)
    both = grouped_sum(both, 2, 2 * levels) / levels
    ends = (lane == 0) | (lane == cols - 1)
    rhs = rhs_in[...] + jnp.where(ends, roll(both, cols - 1 - (6 * levels - 2)), 0.0)
    rhs_out[...] = rhs
    lane_e = lanes_of(east.shape)
    strip = jnp.where(lane_e % 8 < REACH, west, east)
    base = 6 * levels
    first = roll(both, base + REACH - (8 * levels - 2))
    second = roll(both, base + REACH - 1 - (8 * levels - 1))
    body = strip[:rows] + jnp.where(lane == base + REACH, first, 0.0) + jnp.where(lane == base + REACH - 1, second, 0.0)
    strip_out[pl.ds(0, rows), :] = body
    corner = strip[rows:]
    strip_out[pl.ds(rows, TILE), :] = corner
    even = places[3] == 1
    depth = kmt[...].astype(jnp.float32)
    n3 = 3 * levels
    for ref, is_a in ((send_a, True), (send_b, False)):
        up = even if is_a else jnp.logical_not(even)
        ref[pl.ds(0, n3), :] = jnp.where(up, top[...], bottom[...])
        for i, field in enumerate((rhs, depth, fs[...], body)):
            ref[pl.ds(n3 + TILE * i, TILE), :] = jnp.where(up, field[rows - TILE :], field[:TILE])
        ref[pl.ds(n3 + 4 * TILE, TILE), :] = corner


def rows_kernel(places, got_a, got_b, top, bottom, kmt, fs, rhs_in, strip_in, basis, moments):
    rows, cols = kmt.shape
    levels = top.shape[0] // 3
    north, south = sides(places[3] == 1, places[5], places[4], got_a[...], got_b[...])
    n3 = 3 * levels

    def jump(block):
        return block[:levels] - block[levels : 2 * levels]

    def dot(coefficient, value):
        return jnp.sum(coefficient * value, axis=0, keepdims=True) / levels

    top_v, bottom_v = top[...], bottom[...]
    add_top = dot(top_v[2 * levels :], jump(north[:n3]))
    add_bottom = dot(bottom_v[2 * levels :], jump(south[:n3]))
    add_north = dot(north[2 * levels : n3], jump(top_v))
    add_south = dot(south[2 * levels : n3], jump(bottom_v))
    corner = strip_in[pl.ds(rows, TILE), :]
    low, high = corner[:1], corner[1:2]
    c_north, c_south = north[n3 + 4 * TILE : n3 + 4 * TILE + 1], south[n3 + 4 * TILE + 1 : n3 + 4 * TILE + 2]
    half = 8 * levels
    edge = (1, cols)
    lane_1 = lanes_of(edge)

    def cross(coefficient, value):
        product = jnp.where(lane_1 >= half, coefficient * roll(value, half), 0.0)
        summed = grouped_sum(product, 8, 8 * levels) / levels
        return jnp.where((lane_1 // 8) == 6 * levels // 8, roll(summed, 6 * levels - (16 * levels - 8)), 0.0)

    strip_top, strip_bottom = cross(high, c_north), cross(low, c_south)
    strip_north, strip_south = cross(c_north, high), cross(c_south, low)

    extended = (rows + 2 * TILE, cols)
    row = rows_of(extended)
    lane = lanes_of(extended)

    def extend(own, at):
        pieces = [own, north[n3 + TILE * at : n3 + TILE * (at + 1)], south[n3 + TILE * at : n3 + TILE * (at + 1)]]
        return jnp.concatenate(pieces, axis=0)

    def patch(field, at_top, at_bottom, at_north, at_south):
        field = field + jnp.where(row == rows - 1, at_top, 0.0) + jnp.where(row == 0, at_bottom, 0.0)
        return field + jnp.where(row == rows, at_north, 0.0) + jnp.where(row == rows + 2 * TILE - 1, at_south, 0.0)

    rhs_c = patch(extend(rhs_in[...], 0), add_top, add_bottom, add_north, add_south)
    depth_c = extend(kmt[...].astype(jnp.float32), 1)
    free_c = extend(fs[...], 2)
    strip = patch(extend(strip_in[pl.ds(0, rows), :], 3), strip_top, strip_bottom, strip_north, strip_south)
    near = (lane < REACH) | (lane >= cols - REACH)
    base = 6 * levels
    rhs_s, depth_s, free_s = (jnp.where(near, roll(strip, cols - REACH - base - 8 * i), 0.0) for i in range(3))

    scale = 1.0 / HALFWIDTH
    diag_c, side_c = jnp.where(depth_c > 0, (free_c + (4.0 - CENTER)) * scale, 0.0), jnp.where(depth_c > 0, scale, 0.0)
    diag_s, side_s = jnp.where(depth_s > 0, (free_s + (4.0 - CENTER)) * scale, 0.0), jnp.where(depth_s > 0, scale, 0.0)
    right, left = lane == cols - 1, lane == 0

    def apply(c, s):
        rc, rs, lc, ls = roll(c, -1), roll(s, -1), roll(c, 1), roll(s, 1)
        around_c = jnp.where(right, rs, rc) + jnp.where(left, ls, lc) + roll(c, -1, 0) + roll(c, 1, 0)
        around_s = jnp.where(right, rc, rs) + jnp.where(left, lc, ls) + roll(s, -1, 0) + roll(s, 1, 0)
        return diag_c * c - side_c * around_c, diag_s * s - side_s * around_s

    vectors = [(rhs_c, rhs_s)]
    vectors.append(apply(*vectors[0]))
    for _ in range(ITERS - 1):
        c, s = apply(*vectors[-1])
        vectors.append((2.0 * c - vectors[-2][0], 2.0 * s - vectors[-2][1]))
    inner = [c[:rows] for c, _ in vectors]
    line = jnp.zeros(edge, jnp.float32)
    at = 0
    for i in range(ITERS + 1):
        basis[i] = inner[i]
        for j in range(i, ITERS + 1):
            product = (inner[i] * inner[j]).reshape(rows // TILE, TILE, cols).sum(axis=0)
            whole = jnp.sum(jnp.sum(product, axis=0, keepdims=True), axis=1, keepdims=True)
            line = jnp.where(lane_1 == at, whole, line)
            at += 1
    moments[...] = jnp.broadcast_to(line[None], moments.shape)


def times(coefficients):
    out = [None] * (len(coefficients) + 1)

    def put(at, value):
        out[at] = value if out[at] is None else out[at] + value

    for j, c in enumerate(coefficients):
        put(j, CENTER * c)
        if j == 0:
            put(1, HALFWIDTH * c)
        else:
            put(j + 1, 0.5 * HALFWIDTH * c)
            put(j - 1, 0.5 * HALFWIDTH * c)
    return out


def mix(a, b, factor):
    out = []
    for j in range(max(len(a), len(b))):
        if j >= len(b):
            out.append(a[j])
        elif j >= len(a):
            out.append(factor * b[j])
        else:
            out.append(a[j] + factor * b[j])
    return out


def solve_kernel(got, basis, new_in, own, east_west_a, east_west_b, top, bottom, north_south_a, north_south_b, places,
                 surface_out, residual_out, flag, new_out):
    levels = top.shape[0] // 3
    rows, cols = surface_out.shape
    size = ITERS + 1
    line = jnp.sum(got[...], axis=0)
    lane_1 = lanes_of(line.shape)
    gram, at = {}, 0
    for i in range(size):
        for j in range(i, size):
            gram[i, j] = gram[j, i] = jnp.sum(jnp.where(lane_1 == at, line, 0.0), axis=1, keepdims=True)
            at += 1

    def inner(a, b):
        exact = bound = None
        for i, x in enumerate(a):
            for j, y in enumerate(b):
                term = x * y * gram[i, j]
                exact = term if exact is None else exact + term
                bound = jnp.abs(term) if bound is None else bound + jnp.abs(term)
        return exact, bound

    one = jnp.ones_like(gram[0, 0])
    good = one > 0
    residual = [one]
    image = times(residual)
    now, _ = inner(residual, residual)
    product, _ = inner(residual, image)
    alpha = now / product
    direction, along = residual, image
    surface = []
    for step in range(ITERS):
        surface = mix(surface, direction, alpha)
        residual = mix(residual, along, -alpha)
        if step + 1 < ITERS:
            image = times(residual)
            following, bound = inner(residual, residual)
            good = good & (bound <= LIMIT * following)
            product, bound = inner(residual, image)
            good = good & (bound <= LIMIT * product)
            ratio = following / now
            taken = ratio * following / alpha
            good = good & (product + taken <= 0.1 * LIMIT * (product - taken))
            alpha = following / (product - taken)
            direction = mix(residual, direction, ratio)
            along = mix(image, along, ratio)
            now = following
    last, _ = inner(residual, residual)
    good = good & (now <= 0.1 * LIMIT * last)
    vectors = [basis[i] for i in range(size)]
    for ref, combination in ((surface_out, surface), (residual_out, residual)):
        total = combination[0] * vectors[0]
        for j in range(1, len(combination)):
            total = total + combination[j] * vectors[j]
        ref[...] = total
    flag[0, 0] = jnp.where(good, 1, 0)[0, 0]

    shape = (rows, cols)
    lane, row = lanes_of(shape), rows_of(shape)
    east, west = sides(places[0] == 1, places[2], places[1], east_west_a[pl.ds(0, rows), :], east_west_b[pl.ds(0, rows), :])
    north, south = sides(places[3] == 1, places[5], places[4], north_south_a[pl.ds(0, 3 * levels), :], north_south_b[pl.ds(0, 3 * levels), :])
    beyond = jnp.where(lane % 2 == 0, roll(east, -1), roll(west, 1))
    mine = own[pl.ds(0, rows), :]
    ends = (lane == 0) | (lane == cols - 1)
    top_v, bottom_v = top[...], bottom[...]
    for t in range(2):
        added = mine * roll(beyond, 4 * levels - 2 * levels * t)
        above = top_v[2 * levels :] * north[t * levels : (t + 1) * levels]
        below = bottom_v[2 * levels :] * south[t * levels : (t + 1) * levels]
        for k in range(levels):
            value = new_in[t, k] + jnp.where(ends, roll(added, cols - 1 - (4 * levels + 2 * k)), 0.0)
            value = value + jnp.where(row == rows - 1, above[k : k + 1], 0.0) + jnp.where(row == 0, below[k : k + 1], 0.0)
            new_out[t, k] = value


def exchange(first, second, axis):
    peers = lax.axis_size(axis)
    if peers % 2:
        up = [(i, i + 1) for i in range(peers - 1)]
        down = [(j, i) for i, j in up]
        return lax.ppermute(second, axis, down), lax.ppermute(first, axis, up)
    pairs_a = [(i, i ^ 1) for i in range(peers)]
    pairs_b = [(i, (i + 1) % peers if i % 2 else (i - 1) % peers) for i in range(peers)]
    return lax.ppermute(first, axis, pairs_a), lax.ppermute(second, axis, pairs_b)


def place(axis):
    peers, index = lax.axis_size(axis), lax.axis_index(axis)
    even = jnp.int32(1) if peers % 2 else 1 - index % 2
    return [even, index, jnp.int32(peers - 1)]


def padded_2(value, axes, width):
    for axis, dim in axes:
        peers, length = (lax.axis_size(axis), value.shape[dim])
        up = [(i, (i + 1) % peers) for i in range(peers - 1)]
        down = [(j, i) for i, j in up]
        last = lax.slice_in_dim(value, length - width, length, axis=dim)
        first = lax.slice_in_dim(value, 0, width, axis=dim)
        before = lax.ppermute(last, axis, up)
        after = lax.ppermute(first, axis, down)
        value = jnp.concatenate([before, value, after], axis=dim)
    return value


def step_by_step(rhs, kmt, free_surface):
    ocean = (kmt > 0).astype(jnp.float32)
    weight = ocean * (4.0 + free_surface)

    def operate(field):
        padded = padded_2(field, (("by", 0), ("bx", 1)), 1)
        around = padded[1:-1, 2:] + padded[1:-1, :-2] + padded[2:, 1:-1] + padded[:-2, 1:-1]
        return weight * field - ocean * around

    def pair(a, b):
        return lax.psum(lax.psum((jnp.sum(a * a), jnp.sum(a * b)), "bx"), "by")

    surface, residual = jnp.zeros_like(rhs), rhs
    image = operate(residual)
    now, product = pair(residual, image)
    alpha = now / product
    direction, along = residual, image
    for step in range(ITERS):
        surface = surface + alpha * direction
        residual = residual - alpha * along
        if step + 1 < ITERS:
            image = operate(residual)
            following, product = pair(residual, image)
            ratio = following / now
            alpha = following / (product - ratio * following / alpha)
            direction = residual + ratio * direction
            along = image + ratio * along
            now = following
    return surface, residual


def call(kernel, out_shape, kinds, out_kinds=None):
    def spec(kind):
        return pl.BlockSpec(memory_space=pltpu.SMEM if kind == "s" else pltpu.VMEM)

    out_kinds = out_kinds or "v" * len(out_shape)
    return pl.pallas_call(
        kernel,
        out_shape=out_shape,
        in_specs=[spec(k) for k in kinds],
        out_specs=[spec(k) for k in out_kinds],
    )


def f32(*shape):
    return jax.ShapeDtypeStruct(shape, jnp.float32)


def per_device(tracers, velocity, diffusivity, kmt, forcing, free_surface):
    levels = tracers.shape[1]
    rows, cols = kmt.shape
    everyone = lax.axis_size("by") * lax.axis_size("bx")
    places = jnp.stack(place("bx") + place("by")).astype(jnp.int32)
    lines = 3 * levels
    new, packed, top, bottom, rhs = call(
        stencil_kernel,
        [f32(*tracers.shape), f32(rows + TILE, cols), f32(lines, cols), f32(lines, cols), f32(rows, cols)],
        "v" * 6,
    )(tracers, velocity, diffusivity, kmt, forcing, free_surface)
    x_a, x_b = exchange(packed, packed, "bx")
    deep = lines + 5 * TILE
    strip, rhs, send_a, send_b = call(
        columns_kernel,
        [f32(rows + TILE, cols), f32(rows, cols), f32(deep, cols), f32(deep, cols)],
        "s" + "v" * 8,
    )(places, x_a, x_b, packed, top, bottom, kmt, free_surface, rhs)
    y_a, y_b = exchange(send_a, send_b, "by")
    basis, moments = call(
        rows_kernel,
        [f32(ITERS + 1, rows, cols), f32(everyone, 1, cols)],
        "s" + "v" * 8,
    )(places, y_a, y_b, top, bottom, kmt, free_surface, rhs, strip)
    got = lax.all_to_all(moments, ("by", "bx"), 0, 0, tiled=True)
    surface, residual, flag, new_tracers = call(
        solve_kernel,
        [f32(rows, cols), f32(rows, cols), jax.ShapeDtypeStruct((1, 1), jnp.int32), f32(*tracers.shape)],
        "v" * 10 + "s",
        "vvsv",
    )(got, basis, new, packed, x_a, x_b, top, bottom, y_a, y_b, places)
    surface, residual = lax.cond(
        flag[0, 0] == 1,
        lambda: (surface, residual),
        lambda: step_by_step(basis[0], kmt, free_surface),
    )
    return new_tracers, surface, residual


def solution(mesh):
    placed = (
        P(None, None, "by", "bx"),
        P(None, None, "by", "bx"),
        P(None, "by", "bx"),
        P("by", "bx"),
        P("by", "bx"),
        P("by", "bx"),
    )
    return jax.shard_map(
        per_device,
        mesh=mesh,
        in_specs=placed,
        out_specs=(P(None, None, "by", "bx"), P("by", "bx"), P("by", "bx")),
        check_vma=False,
    )
```

```python
import functools

import jax
import jax.numpy as jnp
from jax import lax
from jax.experimental import pallas as pl
from jax.experimental.pallas import tpu as pltpu
from jax.sharding import PartitionSpec as P

ITERS = 4
TILE = 8
REACH = 4
CENTER = 5.0
HALFWIDTH = 4.0
VMEM_GRANT = 12 << 20
LIMIT = 1000.0


def lanes_of(shape):
    return lax.broadcasted_iota(jnp.int32, shape, 1)


def rows_of(shape):
    return lax.broadcasted_iota(jnp.int32, shape, 0)


def roll(value, shift, axis=1):
    size = value.shape[axis]
    shift = shift % size
    return value if shift == 0 else pltpu.roll(value, shift, axis)


def grouped_sum(value, first, last):
    step = first
    while step < last:
        value = value + roll(value, step)
        step *= 2
    return value


def level_terms(kmt, k, di, u, v):
    wet = kmt > k
    mixing = jnp.where(wet, di, 0.0)
    across = jnp.where(wet, 0.5 * u, 0.0)
    along = jnp.where(wet, 0.5 * v, 0.0)
    return wet, 1.0 - 4.0 * mixing, mixing - across, mixing + across, mixing - along, mixing + along


def within(value, own, c_east, c_west, c_north, c_south, lane, row):
    return (
        value * own
        + c_east * roll(value, -1)
        + c_west * roll(value, 1)
        + c_north * roll(value, -1, 0)
        + c_south * roll(value, 1, 0)
    )


def inside(c_east, c_west, c_north, c_south, lane, row):
    rows, cols = lane.shape
    return (
        jnp.where(lane == cols - 1, 0.0, c_east),
        jnp.where(lane == 0, 0.0, c_west),
        jnp.where(row == rows - 1, 0.0, c_north),
        jnp.where(row == 0, 0.0, c_south),
    )


def stencil_kernel(
    tr_hbm, ve_hbm, di_hbm, kmt_hbm, fo_hbm, fs_hbm, packed, top, bottom, rhs_out, tr, ve, di, kmt_ref, fs, fo, sems, flat_sems
):
    levels = tr.shape[1]
    rows, cols = kmt_ref.shape
    shape = (rows, cols)
    flat = [
        pltpu.make_async_copy(source, target, flat_sems.at[i])
        for i, (source, target) in enumerate(((kmt_hbm, kmt_ref), (fs_hbm, fs), (fo_hbm, fo)))
    ]
    for copy in flat:
        copy.start()
    copies = []
    for k in range(levels):
        trio = (
            pltpu.make_async_copy(tr_hbm.at[:, k], tr.at[:, k], sems.at[k, 0]),
            pltpu.make_async_copy(ve_hbm.at[:, k], ve.at[:, k], sems.at[k, 1]),
            pltpu.make_async_copy(di_hbm.at[k], di.at[k], sems.at[k, 2]),
        )
        for copy in trio:
            copy.start()
        copies.append(trio)
    lane, row = lanes_of(shape), rows_of(shape)
    for copy in flat:
        copy.wait()
    kmt = kmt_ref[...]
    base = 6 * levels
    pack = jnp.zeros(shape, jnp.float32)
    for i, field in enumerate((kmt.astype(jnp.float32), fs[...])):
        pack = jnp.where((lane // 8) == base // 8 + 1 + i, roll(field, base + 8 + 8 * i + REACH), pack)
    total = jnp.zeros(shape, jnp.float32)
    for k in range(levels):
        for copy in copies[k]:
            copy.wait()
        wet, own, c_east, c_west, c_north, c_south = level_terms(kmt, k, di[k], ve[0, k], ve[1, k])
        edge = jnp.where(lane == cols - 1, c_east, c_west)
        top[pl.ds(2 * levels + k, 1), :] = c_north[rows - 1 :, :]
        bottom[pl.ds(2 * levels + k, 1), :] = c_south[:1, :]
        pack = jnp.where((lane // 2) == 2 * levels + k, roll(edge, 4 * levels + 2 * k + 1), pack)
        values = [jnp.where(wet, tr[t, k], 0.0) for t in range(2)]
        for t, value in enumerate(values):
            top[pl.ds(t * levels + k, 1), :] = value[rows - 1 :, :]
            bottom[pl.ds(t * levels + k, 1), :] = value[:1, :]
            pack = jnp.where((lane // 2) == t * levels + k, roll(value, 2 * (t * levels + k) + 1), pack)
        total = total + within(values[0] - values[1], own, *inside(c_east, c_west, c_north, c_south, lane, row), lane, row)
    rhs = jnp.where(kmt > 0, fo[...] + total / levels, 0.0)
    rhs_out[...] = rhs
    packed[pl.ds(0, rows), :] = jnp.where((lane // 8) == base // 8, roll(rhs, base + REACH), pack)
    small = (levels, cols)
    lane_s, row_s = lanes_of(small), rows_of(small)
    corner = jnp.zeros((TILE, cols), jnp.float32)
    row_c = rows_of((TILE, cols))
    for i, ref in enumerate((bottom, top)):
        jump = ref[pl.ds(0, levels), :] - ref[pl.ds(levels, levels), :]
        past = ref[pl.ds(2 * levels, levels), :]
        line = jnp.zeros(small, jnp.float32)
        for start, field in ((0, jump), (8 * levels, past)):
            spread = pltpu.roll(field, (start + REACH) % cols, 1, stride=8, stride_axis=0)
            line = line + jnp.where((lane_s // 8) == start // 8 + row_s, spread, 0.0)
        corner = jnp.where(row_c == i, jnp.sum(line, axis=0, keepdims=True), corner)
    packed[pl.ds(rows, TILE), :] = corner


def tracers_kernel(tr, ve, di, kmt_ref, own_ref, east_west_a, east_west_b, top, bottom, north_south_a, north_south_b, new_out):
    levels = tr.shape[1]
    rows, cols = kmt_ref.shape
    shape = (rows, cols)
    lane, row = lanes_of(shape), rows_of(shape)
    kmt = kmt_ref[...]
    east, west = sides("bx", east_west_a[pl.ds(0, rows), :], east_west_b[pl.ds(0, rows), :])
    north, south = sides("by", north_south_a[pl.ds(0, 3 * levels), :], north_south_b[pl.ds(0, 3 * levels), :])
    beyond = jnp.where(lane % 2 == 0, roll(east, -1), roll(west, 1))
    mine = own_ref[pl.ds(0, rows), :]
    ends = (lane == 0) | (lane == cols - 1)
    top_v, bottom_v = top[...], bottom[...]
    added = [mine * roll(beyond, 4 * levels - 2 * levels * t) for t in range(2)]
    above = [top_v[2 * levels :] * north[t * levels : (t + 1) * levels] for t in range(2)]
    below = [bottom_v[2 * levels :] * south[t * levels : (t + 1) * levels] for t in range(2)]
    for k in range(levels):
        wet, own, *around = level_terms(kmt, k, di[k], ve[0, k], ve[1, k])
        around = inside(*around, lane, row)
        for t in range(2):
            value = within(jnp.where(wet, tr[t, k], 0.0), own, *around, lane, row)
            value = value + jnp.where(ends, roll(added[t], cols - 1 - (4 * levels + 2 * k)), 0.0)
            value = value + jnp.where(row == rows - 1, above[t][k : k + 1], 0.0) + jnp.where(row == 0, below[t][k : k + 1], 0.0)
            new_out[t, k] = value


def is_even(axis):
    return lax.axis_index(axis) % 2 == 0 if lax.axis_size(axis) % 2 == 0 else lax.axis_size(axis) > 0


def sides(axis, got_a, got_b):
    index, even = lax.axis_index(axis), is_even(axis)
    after = jnp.where(even, got_a, got_b)
    before = jnp.where(even, got_b, got_a)
    return jnp.where(index < lax.axis_size(axis) - 1, after, 0.0), jnp.where(index > 0, before, 0.0)


def columns_kernel(got_a, got_b, packed, top, bottom, kmt, fs, rhs_in, strip_out, rhs_out, send_a, send_b):
    rows, cols = kmt.shape
    levels = top.shape[0] // 3
    east, west = sides("bx", got_a[...], got_b[...])
    shape = (rows, cols)
    lane = lanes_of(shape)
    mine = packed[pl.ds(0, rows), :]
    e, w = east[:rows], west[:rows]
    beyond = jnp.where(lane % 2 == 0, roll(e, -1), roll(w, 1))
    jump_beyond = roll(beyond, 4 * levels) - roll(beyond, 2 * levels)
    jump_mine = roll(mine, 4 * levels) - roll(mine, 2 * levels)
    here = (lane >= 4 * levels) & (lane < 6 * levels)
    inward = jnp.where(here, mine * jump_beyond, 0.0)
    outward = jnp.where(here, beyond * jump_mine, 0.0)
    both = inward + roll(outward, 2 * levels)
    both = grouped_sum(both, 2, 2 * levels) / levels
    ends = (lane == 0) | (lane == cols - 1)
    rhs = rhs_in[...] + jnp.where(ends, roll(both, cols - 1 - (6 * levels - 2)), 0.0)
    rhs_out[...] = rhs
    lane_e = lanes_of(east.shape)
    strip = jnp.where(lane_e % 8 < REACH, west, east)
    base = 6 * levels
    first = roll(both, base + REACH - (8 * levels - 2))
    second = roll(both, base + REACH - 1 - (8 * levels - 1))
    body = strip[:rows] + jnp.where(lane == base + REACH, first, 0.0) + jnp.where(lane == base + REACH - 1, second, 0.0)
    strip_out[pl.ds(0, rows), :] = body
    corner = strip[rows:]
    strip_out[pl.ds(rows, TILE), :] = corner
    even = is_even("by")
    depth = kmt[...].astype(jnp.float32)
    n3 = 3 * levels
    for ref, is_a in ((send_a, True), (send_b, False)):
        up = even if is_a else jnp.logical_not(even)
        ref[pl.ds(0, n3), :] = jnp.where(up, top[...], bottom[...])
        for i, field in enumerate((rhs, depth, fs[...], body)):
            ref[pl.ds(n3 + TILE * i, TILE), :] = jnp.where(up, field[rows - TILE :], field[:TILE])
        ref[pl.ds(n3 + 4 * TILE, TILE), :] = corner


def rows_kernel(got_a, got_b, top, bottom, kmt, fs, rhs_in, strip_in, basis, moments):
    rows, cols = kmt.shape
    levels = top.shape[0] // 3
    north, south = sides("by", got_a[...], got_b[...])
    n3 = 3 * levels

    def jump(block):
        return block[:levels] - block[levels : 2 * levels]

    def dot(coefficient, value):
        return jnp.sum(coefficient * value, axis=0, keepdims=True) / levels

    top_v, bottom_v = top[...], bottom[...]
    add_top = dot(top_v[2 * levels :], jump(north[:n3]))
    add_bottom = dot(bottom_v[2 * levels :], jump(south[:n3]))
    add_north = dot(north[2 * levels : n3], jump(top_v))
    add_south = dot(south[2 * levels : n3], jump(bottom_v))
    corner = strip_in[pl.ds(rows, TILE), :]
    low, high = corner[:1], corner[1:2]
    c_north, c_south = north[n3 + 4 * TILE : n3 + 4 * TILE + 1], south[n3 + 4 * TILE + 1 : n3 + 4 * TILE + 2]
    half = 8 * levels
    edge = (1, cols)
    lane_1 = lanes_of(edge)

    def cross(coefficient, value):
        product = jnp.where(lane_1 >= half, coefficient * roll(value, half), 0.0)
        summed = grouped_sum(product, 8, 8 * levels) / levels
        return jnp.where((lane_1 // 8) == 6 * levels // 8, roll(summed, 6 * levels - (16 * levels - 8)), 0.0)

    strip_top, strip_bottom = cross(high, c_north), cross(low, c_south)
    strip_north, strip_south = cross(c_north, high), cross(c_south, low)

    extended = (rows + 2 * TILE, cols)
    row = rows_of(extended)
    lane = lanes_of(extended)

    def extend(own, at):
        pieces = [own, north[n3 + TILE * at : n3 + TILE * (at + 1)], south[n3 + TILE * at : n3 + TILE * (at + 1)]]
        return jnp.concatenate(pieces, axis=0)

    def patch(field, at_top, at_bottom, at_north, at_south):
        field = field + jnp.where(row == rows - 1, at_top, 0.0) + jnp.where(row == 0, at_bottom, 0.0)
        return field + jnp.where(row == rows, at_north, 0.0) + jnp.where(row == rows + 2 * TILE - 1, at_south, 0.0)

    rhs_c = patch(extend(rhs_in[...], 0), add_top, add_bottom, add_north, add_south)
    depth_c = extend(kmt[...].astype(jnp.float32), 1)
    free_c = extend(fs[...], 2)
    strip = patch(extend(strip_in[pl.ds(0, rows), :], 3), strip_top, strip_bottom, strip_north, strip_south)
    near = (lane < REACH) | (lane >= cols - REACH)
    base = 6 * levels
    rhs_s, depth_s, free_s = (jnp.where(near, roll(strip, cols - REACH - base - 8 * i), 0.0) for i in range(3))

    scale = 1.0 / HALFWIDTH
    diag_c, side_c = jnp.where(depth_c > 0, (free_c + (4.0 - CENTER)) * scale, 0.0), jnp.where(depth_c > 0, scale, 0.0)
    diag_s, side_s = jnp.where(depth_s > 0, (free_s + (4.0 - CENTER)) * scale, 0.0), jnp.where(depth_s > 0, scale, 0.0)
    right, left = lane == cols - 1, lane == 0

    def apply(c, s):
        rc, rs, lc, ls = roll(c, -1), roll(s, -1), roll(c, 1), roll(s, 1)
        around_c = jnp.where(right, rs, rc) + jnp.where(left, ls, lc) + roll(c, -1, 0) + roll(c, 1, 0)
        around_s = jnp.where(right, rc, rs) + jnp.where(left, lc, ls) + roll(s, -1, 0) + roll(s, 1, 0)
        return diag_c * c - side_c * around_c, diag_s * s - side_s * around_s

    vectors = [(rhs_c, rhs_s)]
    vectors.append(apply(*vectors[0]))
    for _ in range(ITERS - 1):
        c, s = apply(*vectors[-1])
        vectors.append((2.0 * c - vectors[-2][0], 2.0 * s - vectors[-2][1]))
    inner = [c[:rows] for c, _ in vectors]
    line = jnp.zeros(edge, jnp.float32)
    at = 0
    for i in range(ITERS + 1):
        basis[i] = inner[i]
        for j in range(i, ITERS + 1):
            product = (inner[i] * inner[j]).reshape(rows // TILE, TILE, cols).sum(axis=0)
            whole = jnp.sum(jnp.sum(product, axis=0, keepdims=True), axis=1, keepdims=True)
            line = jnp.where(lane_1 == at, whole, line)
            at += 1
    moments[...] = jnp.broadcast_to(line[None], moments.shape)


def times(coefficients):
    out = [None] * (len(coefficients) + 1)

    def put(at, value):
        out[at] = value if out[at] is None else out[at] + value

    for j, c in enumerate(coefficients):
        put(j, CENTER * c)
        if j == 0:
            put(1, HALFWIDTH * c)
        else:
            put(j + 1, 0.5 * HALFWIDTH * c)
            put(j - 1, 0.5 * HALFWIDTH * c)
    return out


def mix(a, b, factor):
    out = []
    for j in range(max(len(a), len(b))):
        if j >= len(b):
            out.append(a[j])
        elif j >= len(a):
            out.append(factor * b[j])
        else:
            out.append(a[j] + factor * b[j])
    return out


def solve_kernel(got, basis, surface_out, residual_out, flag):
    size = ITERS + 1
    line = jnp.sum(got[...], axis=0)
    lane_1 = lanes_of(line.shape)
    gram, at = {}, 0
    for i in range(size):
        for j in range(i, size):
            gram[i, j] = gram[j, i] = jnp.sum(jnp.where(lane_1 == at, line, 0.0), axis=1, keepdims=True)
            at += 1

    def inner(a, b):
        exact = bound = None
        for i, x in enumerate(a):
            for j, y in enumerate(b):
                term = x * y * gram[i, j]
                exact = term if exact is None else exact + term
                bound = jnp.abs(term) if bound is None else bound + jnp.abs(term)
        return exact, bound

    one = jnp.ones_like(gram[0, 0])
    good = one > 0
    residual = [one]
    image = times(residual)
    now, _ = inner(residual, residual)
    product, _ = inner(residual, image)
    alpha = now / product
    direction, along = residual, image
    surface = []
    for step in range(ITERS):
        surface = mix(surface, direction, alpha)
        residual = mix(residual, along, -alpha)
        if step + 1 < ITERS:
            image = times(residual)
            following, bound = inner(residual, residual)
            good = good & (bound <= LIMIT * following)
            product, bound = inner(residual, image)
            good = good & (bound <= LIMIT * product)
            ratio = following / now
            taken = ratio * following / alpha
            good = good & (product + taken <= 0.1 * LIMIT * (product - taken))
            alpha = following / (product - taken)
            direction = mix(residual, direction, ratio)
            along = mix(image, along, ratio)
            now = following
    last, _ = inner(residual, residual)
    good = good & (now <= 0.1 * LIMIT * last)
    vectors = [basis[i] for i in range(size)]
    for ref, combination in ((surface_out, surface), (residual_out, residual)):
        total = combination[0] * vectors[0]
        for j in range(1, len(combination)):
            total = total + combination[j] * vectors[j]
        ref[...] = total
    flag[0, 0] = jnp.where(good, 1, 0)[0, 0]


def exchange(first, second, axis):
    peers = lax.axis_size(axis)
    if peers % 2:
        up = [(i, i + 1) for i in range(peers - 1)]
        down = [(j, i) for i, j in up]
        return lax.ppermute(second, axis, down), lax.ppermute(first, axis, up)
    pairs_a = [(i, i ^ 1) for i in range(peers)]
    pairs_b = [(i, (i + 1) % peers if i % 2 else (i - 1) % peers) for i in range(peers)]
    return lax.ppermute(first, axis, pairs_a), lax.ppermute(second, axis, pairs_b)


def padded_2(value, axes, width):
    for axis, dim in axes:
        peers, length = (lax.axis_size(axis), value.shape[dim])
        up = [(i, (i + 1) % peers) for i in range(peers - 1)]
        down = [(j, i) for i, j in up]
        last = lax.slice_in_dim(value, length - width, length, axis=dim)
        first = lax.slice_in_dim(value, 0, width, axis=dim)
        before = lax.ppermute(last, axis, up)
        after = lax.ppermute(first, axis, down)
        value = jnp.concatenate([before, value, after], axis=dim)
    return value


def step_by_step(rhs, kmt, free_surface):
    ocean = (kmt > 0).astype(jnp.float32)
    weight = ocean * (4.0 + free_surface)

    def operate(field):
        padded = padded_2(field, (("by", 0), ("bx", 1)), 1)
        around = padded[1:-1, 2:] + padded[1:-1, :-2] + padded[2:, 1:-1] + padded[:-2, 1:-1]
        return weight * field - ocean * around

    def pair(a, b):
        return lax.psum(lax.psum((jnp.sum(a * a), jnp.sum(a * b)), "bx"), "by")

    surface, residual = jnp.zeros_like(rhs), rhs
    image = operate(residual)
    now, product = pair(residual, image)
    alpha = now / product
    direction, along = residual, image
    for step in range(ITERS):
        surface = surface + alpha * direction
        residual = residual - alpha * along
        if step + 1 < ITERS:
            image = operate(residual)
            following, product = pair(residual, image)
            ratio = following / now
            alpha = following / (product - ratio * following / alpha)
            direction = residual + ratio * direction
            along = image + ratio * along
            now = following
    return surface, residual


def call(kernel, out_shape, kinds, out_kinds=None, scratch=(), cost=None, resident=True):
    spaces = {"s": pltpu.SMEM, "v": pltpu.VMEM, "h": pltpu.HBM}
    out_kinds = out_kinds or "v" * len(out_shape)
    if resident:
        out_shape = [spaces[k](o.shape, o.dtype) for k, o in zip(out_kinds, out_shape)]
    return pl.pallas_call(
        kernel,
        out_shape=out_shape,
        in_specs=[pl.BlockSpec(memory_space=spaces[k]) for k in kinds],
        out_specs=[pl.BlockSpec(memory_space=spaces[k]) for k in out_kinds],
        scratch_shapes=scratch,
        cost_estimate=cost,
        compiler_params=pltpu.CompilerParams(vmem_limit_bytes=VMEM_GRANT),
    )


def f32(*shape):
    return jax.ShapeDtypeStruct(shape, jnp.float32)


def per_device(*inputs):
    tracers, velocity, diffusivity, kmt, forcing, free_surface = inputs
    levels = tracers.shape[1]
    rows, cols = kmt.shape
    everyone = lax.axis_size("by") * lax.axis_size("bx")
    lines = 3 * levels
    packed, top, bottom, rhs, tracers, velocity, diffusivity, kmt, free_surface = call(
        stencil_kernel,
        [f32(rows + TILE, cols), f32(lines, cols), f32(lines, cols), f32(rows, cols)]
        + [jax.ShapeDtypeStruct(v.shape, v.dtype) for v in (tracers, velocity, diffusivity, kmt, free_surface)],
        "h" * 6,
        scratch=[
            pltpu.VMEM((rows, cols), jnp.float32),
            pltpu.SemaphoreType.DMA((levels, 3)),
            pltpu.SemaphoreType.DMA((3,)),
        ],
    )(*[pltpu.with_memory_space_constraint(v, pltpu.HBM) for v in inputs])
    x_a, x_b = exchange(packed, packed, "bx")
    deep = lines + 5 * TILE
    strip, rhs, send_a, send_b = call(
        columns_kernel,
        [f32(rows + TILE, cols), f32(rows, cols), f32(deep, cols), f32(deep, cols)],
        "v" * 8,
    )(x_a, x_b, packed, top, bottom, kmt, free_surface, rhs)
    y_a, y_b = exchange(send_a, send_b, "by")
    basis, moments = call(
        rows_kernel,
        [f32(ITERS + 1, rows, cols), f32(everyone, 1, cols)],
        "v" * 8,
    )(y_a, y_b, top, bottom, kmt, free_surface, rhs, strip)
    got = lax.all_to_all(moments, ("by", "bx"), 0, 0, tiled=True)
    new_tracers, = call(
        tracers_kernel,
        [f32(*tracers.shape)],
        "v" * 11,
        resident=False,
        cost=pl.CostEstimate(flops=30 * tracers.size, bytes_accessed=16 * tracers.size, transcendentals=0),
    )(tracers, velocity, diffusivity, kmt, packed, x_a, x_b, top, bottom, y_a, y_b)
    surface, residual, flag = call(
        solve_kernel,
        [f32(rows, cols), f32(rows, cols), jax.ShapeDtypeStruct((1, 1), jnp.int32)],
        "vv",
        "vvs",
    )(got, basis)
    surface, residual = lax.cond(
        flag[0, 0] == 1,
        lambda: (surface, residual),
        lambda: step_by_step(basis[0], kmt, free_surface),
    )
    return new_tracers, surface, residual


def solution(mesh):
    placed = (
        P(None, None, "by", "bx"),
        P(None, None, "by", "bx"),
        P(None, "by", "bx"),
        P("by", "bx"),
        P("by", "bx"),
        P("by", "bx"),
    )
    return jax.shard_map(
        per_device,
        mesh=mesh,
        in_specs=placed,
        out_specs=(P(None, None, "by", "bx"), P("by", "bx"), P("by", "bx")),
        check_vma=False,
    )
```

```python
import functools

import jax
import jax.numpy as jnp
from jax import lax
from jax.experimental import pallas as pl
from jax.experimental.pallas import tpu as pltpu
from jax.sharding import PartitionSpec as P

ITERS = 4
TILE = 8
REACH = 4
CENTER = 5.0
HALFWIDTH = 4.0
VMEM_GRANT = 12 << 20
CHUNK = 48
LIMIT = 1000.0


def lanes_of(shape):
    return lax.broadcasted_iota(jnp.int32, shape, 1)


def rows_of(shape):
    return lax.broadcasted_iota(jnp.int32, shape, 0)


def roll(value, shift, axis=1):
    size = value.shape[axis]
    shift = shift % size
    return value if shift == 0 else pltpu.roll(value, shift, axis)


def grouped_sum(value, first, last):
    step = first
    while step < last:
        value = value + roll(value, step)
        step *= 2
    return value


def level_terms(kmt, k, di, u, v):
    wet = kmt > k
    mixing = jnp.where(wet, di, 0.0)
    across = jnp.where(wet, 0.5 * u, 0.0)
    along = jnp.where(wet, 0.5 * v, 0.0)
    return wet, 1.0 - 4.0 * mixing, mixing - across, mixing + across, mixing - along, mixing + along


def within(value, own, c_east, c_west, c_north, c_south, lane, row):
    return (
        value * own
        + c_east * roll(value, -1)
        + c_west * roll(value, 1)
        + c_north * roll(value, -1, 0)
        + c_south * roll(value, 1, 0)
    )


def inside(c_east, c_west, c_north, c_south, lane, row):
    rows, cols = lane.shape
    return (
        jnp.where(lane == cols - 1, 0.0, c_east),
        jnp.where(lane == 0, 0.0, c_west),
        jnp.where(row == rows - 1, 0.0, c_north),
        jnp.where(row == 0, 0.0, c_south),
    )


def stencil_kernel(
    tr_hbm, ve_hbm, di_hbm, kmt_hbm, fo_hbm, fs_hbm, packed, top, bottom, rhs_out, tr, ve, di, kmt_ref, fs, fo, sems, flat_sems
):
    levels = tr.shape[1]
    rows, cols = kmt_ref.shape
    chunk = CHUNK if rows % CHUNK == 0 else rows
    flat = [
        pltpu.make_async_copy(source, target, flat_sems.at[i])
        for i, (source, target) in enumerate(((kmt_hbm, kmt_ref), (fs_hbm, fs), (fo_hbm, fo)))
    ]
    for copy in flat:
        copy.start()
    copies = []
    for c in range(rows // chunk):
        part = pl.ds(c * chunk, chunk)
        trio = (
            pltpu.make_async_copy(tr_hbm.at[:, :, part], tr.at[:, :, part], sems.at[c, 0]),
            pltpu.make_async_copy(ve_hbm.at[:, :, part], ve.at[:, :, part], sems.at[c, 1]),
            pltpu.make_async_copy(di_hbm.at[:, part], di.at[:, part], sems.at[c, 2]),
        )
        for copy in trio:
            copy.start()
        copies.append(trio)
    shape = (chunk, cols)
    lane, row = lanes_of(shape), rows_of(shape)
    base = 6 * levels
    first, last = lane == 0, lane == cols - 1
    lean = jnp.where(last, -0.5, 0.5)
    for copy in flat:
        copy.wait()
    ready = 0
    for c in range(rows // chunk):
        start = c * chunk
        while ready < min(c + 2, rows // chunk):
            for copy in copies[ready]:
                copy.wait()
            ready += 1
        part = pl.ds(start, chunk)
        kmt = kmt_ref[part, :]
        pack = jnp.zeros(shape, jnp.float32)
        for i, field in enumerate((kmt.astype(jnp.float32), fs[part, :])):
            pack = jnp.where((lane // 8) == base // 8 + 1 + i, roll(field, base + 8 + 8 * i + REACH), pack)
        mixed = jnp.zeros(shape, jnp.float32)
        carried = jnp.zeros(shape, jnp.float32)

        def row_jump(k, at):
            if at < 0 or at >= rows:
                return jnp.zeros((1, cols), jnp.float32)
            one = pl.ds(at, 1)
            return jnp.where(kmt_ref[one, :] > k, tr[0, k, one, :] - tr[1, k, one, :], 0.0)

        for k in range(levels):
            wet = kmt > k
            values = [jnp.where(wet, tr[t, k, part, :], 0.0) for t in range(2)]
            mixing, u, v = di[k, part, :], ve[0, k, part, :], ve[1, k, part, :]
            edge = jnp.where(wet, mixing + lean * u, 0.0)
            for i, field in enumerate((*values, edge)):
                slot = i * levels + k
                pack = jnp.where((lane // 2) == slot, roll(field, 2 * slot + 1), pack)
            jump = values[0] - values[1]
            east = jnp.where(last, 0.0, roll(jump, -1))
            west = jnp.where(first, 0.0, roll(jump, 1))
            north = jnp.where(row == chunk - 1, row_jump(k, start + chunk), roll(jump, -1, 0))
            south = jnp.where(row == 0, row_jump(k, start - 1), roll(jump, 1, 0))
            around = (east + west) + (north + south) - 4.0 * jump
            mixed = mixed + jnp.where(wet, jump + mixing * around, 0.0)
            carried = carried + jnp.where(wet, u * (east - west) + v * (north - south), 0.0)
            for ref, at, sign in ((bottom, 0, 0.5), (top, rows - 1, -0.5)):
                if start <= at < start + chunk:
                    here = slice(at - start, at - start + 1)
                    for i, field in enumerate(values):
                        ref[pl.ds(i * levels + k, 1), :] = field[here]
                    ref[pl.ds(2 * levels + k, 1), :] = jnp.where(wet[here], mixing[here] + sign * v[here], 0.0)
        rhs = jnp.where(kmt > 0, fo[part, :] + (mixed - 0.5 * carried) / levels, 0.0)
        rhs_out[part, :] = rhs
        packed[part, :] = jnp.where((lane // 8) == base // 8, roll(rhs, base + REACH), pack)
    small = (levels, cols)
    lane_s, row_s = lanes_of(small), rows_of(small)
    corner = jnp.zeros((TILE, cols), jnp.float32)
    row_c = rows_of((TILE, cols))
    for i, ref in enumerate((bottom, top)):
        jump = ref[pl.ds(0, levels), :] - ref[pl.ds(levels, levels), :]
        past = ref[pl.ds(2 * levels, levels), :]
        line = jnp.zeros(small, jnp.float32)
        for start, field in ((0, jump), (8 * levels, past)):
            spread = pltpu.roll(field, (start + REACH) % cols, 1, stride=8, stride_axis=0)
            line = line + jnp.where((lane_s // 8) == start // 8 + row_s, spread, 0.0)
        corner = jnp.where(row_c == i, jnp.sum(line, axis=0, keepdims=True), corner)
    packed[pl.ds(rows, TILE), :] = corner


def tracers_kernel(tr, ve, di, kmt_ref, own_ref, east_west_a, east_west_b, top, bottom, north_south_a, north_south_b, new_out):
    levels = tr.shape[1]
    rows, cols = kmt_ref.shape
    shape = (rows, cols)
    lane, row = lanes_of(shape), rows_of(shape)
    kmt = kmt_ref[...]
    east, west = sides("bx", east_west_a[pl.ds(0, rows), :], east_west_b[pl.ds(0, rows), :])
    north, south = sides("by", north_south_a[pl.ds(0, 3 * levels), :], north_south_b[pl.ds(0, 3 * levels), :])
    beyond = jnp.where(lane % 2 == 0, roll(east, -1), roll(west, 1))
    mine = own_ref[pl.ds(0, rows), :]
    ends = (lane == 0) | (lane == cols - 1)
    top_v, bottom_v = top[...], bottom[...]
    added = [mine * roll(beyond, 4 * levels - 2 * levels * t) for t in range(2)]
    above = [top_v[2 * levels :] * north[t * levels : (t + 1) * levels] for t in range(2)]
    below = [bottom_v[2 * levels :] * south[t * levels : (t + 1) * levels] for t in range(2)]
    for k in range(levels):
        wet, own, *around = level_terms(kmt, k, di[k], ve[0, k], ve[1, k])
        around = inside(*around, lane, row)
        for t in range(2):
            value = within(jnp.where(wet, tr[t, k], 0.0), own, *around, lane, row)
            value = value + jnp.where(ends, roll(added[t], cols - 1 - (4 * levels + 2 * k)), 0.0)
            value = value + jnp.where(row == rows - 1, above[t][k : k + 1], 0.0) + jnp.where(row == 0, below[t][k : k + 1], 0.0)
            new_out[t, k] = value


def is_even(axis):
    return lax.axis_index(axis) % 2 == 0 if lax.axis_size(axis) % 2 == 0 else lax.axis_size(axis) > 0


def sides(axis, got_a, got_b):
    index, even = lax.axis_index(axis), is_even(axis)
    after = jnp.where(even, got_a, got_b)
    before = jnp.where(even, got_b, got_a)
    return jnp.where(index < lax.axis_size(axis) - 1, after, 0.0), jnp.where(index > 0, before, 0.0)


def columns_kernel(got_a, got_b, packed, top, bottom, kmt, fs, rhs_in, strip_out, rhs_out, send_a, send_b):
    rows, cols = kmt.shape
    levels = top.shape[0] // 3
    east, west = sides("bx", got_a[...], got_b[...])
    shape = (rows, cols)
    lane = lanes_of(shape)
    mine = packed[pl.ds(0, rows), :]
    e, w = east[:rows], west[:rows]
    beyond = jnp.where(lane % 2 == 0, roll(e, -1), roll(w, 1))
    jump_beyond = roll(beyond, 4 * levels) - roll(beyond, 2 * levels)
    jump_mine = roll(mine, 4 * levels) - roll(mine, 2 * levels)
    here = (lane >= 4 * levels) & (lane < 6 * levels)
    inward = jnp.where(here, mine * jump_beyond, 0.0)
    outward = jnp.where(here, beyond * jump_mine, 0.0)
    both = inward + roll(outward, 2 * levels)
    both = grouped_sum(both, 2, 2 * levels) / levels
    ends = (lane == 0) | (lane == cols - 1)
    rhs = rhs_in[...] + jnp.where(ends, roll(both, cols - 1 - (6 * levels - 2)), 0.0)
    rhs_out[...] = rhs
    lane_e = lanes_of(east.shape)
    strip = jnp.where(lane_e % 8 < REACH, west, east)
    base = 6 * levels
    first = roll(both, base + REACH - (8 * levels - 2))
    second = roll(both, base + REACH - 1 - (8 * levels - 1))
    body = strip[:rows] + jnp.where(lane == base + REACH, first, 0.0) + jnp.where(lane == base + REACH - 1, second, 0.0)
    strip_out[pl.ds(0, rows), :] = body
    corner = strip[rows:]
    strip_out[pl.ds(rows, TILE), :] = corner
    even = is_even("by")
    depth = kmt[...].astype(jnp.float32)
    n3 = 3 * levels
    for ref, is_a in ((send_a, True), (send_b, False)):
        up = even if is_a else jnp.logical_not(even)
        ref[pl.ds(0, n3), :] = jnp.where(up, top[...], bottom[...])
        for i, field in enumerate((rhs, depth, fs[...], body)):
            ref[pl.ds(n3 + TILE * i, TILE), :] = jnp.where(up, field[rows - TILE :], field[:TILE])
        ref[pl.ds(n3 + 4 * TILE, TILE), :] = corner


def rows_kernel(got_a, got_b, top, bottom, kmt, fs, rhs_in, strip_in, basis, moments):
    rows, cols = kmt.shape
    levels = top.shape[0] // 3
    north, south = sides("by", got_a[...], got_b[...])
    n3 = 3 * levels

    def jump(block):
        return block[:levels] - block[levels : 2 * levels]

    def dot(coefficient, value):
        return jnp.sum(coefficient * value, axis=0, keepdims=True) / levels

    top_v, bottom_v = top[...], bottom[...]
    add_top = dot(top_v[2 * levels :], jump(north[:n3]))
    add_bottom = dot(bottom_v[2 * levels :], jump(south[:n3]))
    add_north = dot(north[2 * levels : n3], jump(top_v))
    add_south = dot(south[2 * levels : n3], jump(bottom_v))
    corner = strip_in[pl.ds(rows, TILE), :]
    low, high = corner[:1], corner[1:2]
    c_north, c_south = north[n3 + 4 * TILE : n3 + 4 * TILE + 1], south[n3 + 4 * TILE + 1 : n3 + 4 * TILE + 2]
    half = 8 * levels
    edge = (1, cols)
    lane_1 = lanes_of(edge)

    def cross(coefficient, value):
        product = jnp.where(lane_1 >= half, coefficient * roll(value, half), 0.0)
        summed = grouped_sum(product, 8, 8 * levels) / levels
        return jnp.where((lane_1 // 8) == 6 * levels // 8, roll(summed, 6 * levels - (16 * levels - 8)), 0.0)

    strip_top, strip_bottom = cross(high, c_north), cross(low, c_south)
    strip_north, strip_south = cross(c_north, high), cross(c_south, low)

    extended = (rows + 2 * TILE, cols)
    row = rows_of(extended)
    lane = lanes_of(extended)

    def extend(own, at):
        pieces = [own, north[n3 + TILE * at : n3 + TILE * (at + 1)], south[n3 + TILE * at : n3 + TILE * (at + 1)]]
        return jnp.concatenate(pieces, axis=0)

    def patch(field, at_top, at_bottom, at_north, at_south):
        field = field + jnp.where(row == rows - 1, at_top, 0.0) + jnp.where(row == 0, at_bottom, 0.0)
        return field + jnp.where(row == rows, at_north, 0.0) + jnp.where(row == rows + 2 * TILE - 1, at_south, 0.0)

    rhs_c = patch(extend(rhs_in[...], 0), add_top, add_bottom, add_north, add_south)
    depth_c = extend(kmt[...].astype(jnp.float32), 1)
    free_c = extend(fs[...], 2)
    strip = patch(extend(strip_in[pl.ds(0, rows), :], 3), strip_top, strip_bottom, strip_north, strip_south)
    near = (lane < REACH) | (lane >= cols - REACH)
    base = 6 * levels
    rhs_s, depth_s, free_s = (jnp.where(near, roll(strip, cols - REACH - base - 8 * i), 0.0) for i in range(3))

    scale = 1.0 / HALFWIDTH
    diag_c, side_c = jnp.where(depth_c > 0, (free_c + (4.0 - CENTER)) * scale, 0.0), jnp.where(depth_c > 0, scale, 0.0)
    diag_s, side_s = jnp.where(depth_s > 0, (free_s + (4.0 - CENTER)) * scale, 0.0), jnp.where(depth_s > 0, scale, 0.0)
    right, left = lane == cols - 1, lane == 0

    def apply(c, s):
        rc, rs, lc, ls = roll(c, -1), roll(s, -1), roll(c, 1), roll(s, 1)
        around_c = jnp.where(right, rs, rc) + jnp.where(left, ls, lc) + roll(c, -1, 0) + roll(c, 1, 0)
        around_s = jnp.where(right, rc, rs) + jnp.where(left, lc, ls) + roll(s, -1, 0) + roll(s, 1, 0)
        return diag_c * c - side_c * around_c, diag_s * s - side_s * around_s

    vectors = [(rhs_c, rhs_s)]
    vectors.append(apply(*vectors[0]))
    for _ in range(ITERS - 1):
        c, s = apply(*vectors[-1])
        vectors.append((2.0 * c - vectors[-2][0], 2.0 * s - vectors[-2][1]))
    inner = [c[:rows] for c, _ in vectors]
    line = jnp.zeros(edge, jnp.float32)
    at = 0
    for i in range(ITERS + 1):
        basis[i] = inner[i]
        for j in range(i, ITERS + 1):
            product = (inner[i] * inner[j]).reshape(rows // TILE, TILE, cols).sum(axis=0)
            whole = jnp.sum(jnp.sum(product, axis=0, keepdims=True), axis=1, keepdims=True)
            line = jnp.where(lane_1 == at, whole, line)
            at += 1
    moments[...] = jnp.broadcast_to(line[None], moments.shape)


def times(coefficients):
    out = [None] * (len(coefficients) + 1)

    def put(at, value):
        out[at] = value if out[at] is None else out[at] + value

    for j, c in enumerate(coefficients):
        put(j, CENTER * c)
        if j == 0:
            put(1, HALFWIDTH * c)
        else:
            put(j + 1, 0.5 * HALFWIDTH * c)
            put(j - 1, 0.5 * HALFWIDTH * c)
    return out


def mix(a, b, factor):
    out = []
    for j in range(max(len(a), len(b))):
        if j >= len(b):
            out.append(a[j])
        elif j >= len(a):
            out.append(factor * b[j])
        else:
            out.append(a[j] + factor * b[j])
    return out


def solve_kernel(got, basis, surface_out, residual_out, flag, results, sems):
    size = ITERS + 1
    line = jnp.sum(got[...], axis=0)
    lane_1 = lanes_of(line.shape)
    gram, at = {}, 0
    for i in range(size):
        for j in range(i, size):
            gram[i, j] = gram[j, i] = jnp.sum(jnp.where(lane_1 == at, line, 0.0), axis=1, keepdims=True)
            at += 1

    def inner(a, b):
        exact = bound = None
        for i, x in enumerate(a):
            for j, y in enumerate(b):
                term = x * y * gram[i, j]
                exact = term if exact is None else exact + term
                bound = jnp.abs(term) if bound is None else bound + jnp.abs(term)
        return exact, bound

    one = jnp.ones_like(gram[0, 0])
    good = one > 0
    residual = [one]
    image = times(residual)
    now, _ = inner(residual, residual)
    product, _ = inner(residual, image)
    alpha = now / product
    direction, along = residual, image
    surface = []
    for step in range(ITERS):
        surface = mix(surface, direction, alpha)
        residual = mix(residual, along, -alpha)
        if step + 1 < ITERS:
            image = times(residual)
            following, bound = inner(residual, residual)
            good = good & (bound <= LIMIT * following)
            product, bound = inner(residual, image)
            good = good & (bound <= LIMIT * product)
            ratio = following / now
            taken = ratio * following / alpha
            good = good & (product + taken <= 0.1 * LIMIT * (product - taken))
            alpha = following / (product - taken)
            direction = mix(residual, direction, ratio)
            along = mix(image, along, ratio)
            now = following
    last, _ = inner(residual, residual)
    good = good & (now <= 0.1 * LIMIT * last)
    vectors = [basis[i] for i in range(size)]
    copies = []
    for at, (ref, combination) in enumerate(((surface_out, surface), (residual_out, residual))):
        total = combination[0] * vectors[0]
        for j in range(1, len(combination)):
            total = total + combination[j] * vectors[j]
        results[at] = total
        copies.append(pltpu.make_async_copy(results.at[at], ref, sems.at[at]))
        copies[at].start()
    flag[0, 0] = jnp.where(good, 1, 0)[0, 0]
    for copy in copies:
        copy.wait()


def exchange(first, second, axis):
    peers = lax.axis_size(axis)
    if peers % 2:
        up = [(i, i + 1) for i in range(peers - 1)]
        down = [(j, i) for i, j in up]
        return lax.ppermute(second, axis, down), lax.ppermute(first, axis, up)
    pairs_a = [(i, i ^ 1) for i in range(peers)]
    pairs_b = [(i, (i + 1) % peers if i % 2 else (i - 1) % peers) for i in range(peers)]
    return lax.ppermute(first, axis, pairs_a), lax.ppermute(second, axis, pairs_b)


def padded_2(value, axes, width):
    for axis, dim in axes:
        peers, length = (lax.axis_size(axis), value.shape[dim])
        up = [(i, (i + 1) % peers) for i in range(peers - 1)]
        down = [(j, i) for i, j in up]
        last = lax.slice_in_dim(value, length - width, length, axis=dim)
        first = lax.slice_in_dim(value, 0, width, axis=dim)
        before = lax.ppermute(last, axis, up)
        after = lax.ppermute(first, axis, down)
        value = jnp.concatenate([before, value, after], axis=dim)
    return value


def step_by_step(rhs, kmt, free_surface):
    ocean = (kmt > 0).astype(jnp.float32)
    weight = ocean * (4.0 + free_surface)

    def operate(field):
        padded = padded_2(field, (("by", 0), ("bx", 1)), 1)
        around = padded[1:-1, 2:] + padded[1:-1, :-2] + padded[2:, 1:-1] + padded[:-2, 1:-1]
        return weight * field - ocean * around

    def pair(a, b):
        return lax.psum(lax.psum((jnp.sum(a * a), jnp.sum(a * b)), "bx"), "by")

    surface, residual = jnp.zeros_like(rhs), rhs
    image = operate(residual)
    now, product = pair(residual, image)
    alpha = now / product
    direction, along = residual, image
    for step in range(ITERS):
        surface = surface + alpha * direction
        residual = residual - alpha * along
        if step + 1 < ITERS:
            image = operate(residual)
            following, product = pair(residual, image)
            ratio = following / now
            alpha = following / (product - ratio * following / alpha)
            direction = residual + ratio * direction
            along = image + ratio * along
            now = following
    return surface, residual


def call(kernel, out_shape, kinds, out_kinds=None, scratch=(), cost=None, resident=True):
    spaces = {"s": pltpu.SMEM, "v": pltpu.VMEM, "h": pltpu.HBM}
    out_kinds = out_kinds or "v" * len(out_shape)
    if resident:
        out_shape = [spaces[k](o.shape, o.dtype) for k, o in zip(out_kinds, out_shape)]
    return pl.pallas_call(
        kernel,
        out_shape=out_shape,
        in_specs=[pl.BlockSpec(memory_space=spaces[k]) for k in kinds],
        out_specs=[pl.BlockSpec(memory_space=spaces[k]) for k in out_kinds],
        scratch_shapes=scratch,
        cost_estimate=cost,
        compiler_params=pltpu.CompilerParams(vmem_limit_bytes=VMEM_GRANT),
    )


def f32(*shape):
    return jax.ShapeDtypeStruct(shape, jnp.float32)


def per_device(*inputs):
    tracers, velocity, diffusivity, kmt, forcing, free_surface = inputs
    levels = tracers.shape[1]
    rows, cols = kmt.shape
    everyone = lax.axis_size("by") * lax.axis_size("bx")
    lines = 3 * levels
    packed, top, bottom, rhs, tracers, velocity, diffusivity, kmt, free_surface = call(
        stencil_kernel,
        [f32(rows + TILE, cols), f32(lines, cols), f32(lines, cols), f32(rows, cols)]
        + [jax.ShapeDtypeStruct(v.shape, v.dtype) for v in (tracers, velocity, diffusivity, kmt, free_surface)],
        "h" * 6,
        scratch=[
            pltpu.VMEM((rows, cols), jnp.float32),
            pltpu.SemaphoreType.DMA((max(rows // CHUNK, 1), 3)),
            pltpu.SemaphoreType.DMA((3,)),
        ],
    )(*[pltpu.with_memory_space_constraint(v, pltpu.HBM) for v in inputs])
    x_a, x_b = exchange(packed, packed, "bx")
    deep = lines + 5 * TILE
    strip, rhs, send_a, send_b = call(
        columns_kernel,
        [f32(rows + TILE, cols), f32(rows, cols), f32(deep, cols), f32(deep, cols)],
        "v" * 8,
    )(x_a, x_b, packed, top, bottom, kmt, free_surface, rhs)
    y_a, y_b = exchange(send_a, send_b, "by")
    basis, moments = call(
        rows_kernel,
        [f32(ITERS + 1, rows, cols), f32(everyone, 1, cols)],
        "v" * 8,
    )(y_a, y_b, top, bottom, kmt, free_surface, rhs, strip)
    got = lax.all_to_all(moments, ("by", "bx"), 0, 0, tiled=True)
    new_tracers, = call(
        tracers_kernel,
        [f32(*tracers.shape)],
        "v" * 11,
        resident=False,
        cost=pl.CostEstimate(flops=30 * tracers.size, bytes_accessed=16 * tracers.size, transcendentals=0),
    )(tracers, velocity, diffusivity, kmt, packed, x_a, x_b, top, bottom, y_a, y_b)
    surface, residual, flag = call(
        solve_kernel,
        [f32(rows, cols), f32(rows, cols), jax.ShapeDtypeStruct((1, 1), jnp.int32)],
        "vv",
        "hhs",
        scratch=[pltpu.VMEM((2, rows, cols), jnp.float32), pltpu.SemaphoreType.DMA((2,))],
    )(got, basis)
    surface, residual = lax.cond(
        flag[0, 0] == 1,
        lambda: (surface, residual),
        lambda: step_by_step(basis[0], kmt, free_surface),
    )
    return new_tracers, surface, residual


def solution(mesh):
    placed = (
        P(None, None, "by", "bx"),
        P(None, None, "by", "bx"),
        P(None, "by", "bx"),
        P("by", "bx"),
        P("by", "bx"),
        P("by", "bx"),
    )
    return jax.shard_map(
        per_device,
        mesh=mesh,
        in_specs=placed,
        out_specs=(P(None, None, "by", "bx"), P("by", "bx"), P("by", "bx")),
        check_vma=False,
    )
```

```python
import jax
import jax.numpy as jnp
from jax import lax
from jax.experimental import pallas as pl
from jax.experimental.pallas import tpu as pltpu
from jax.sharding import PartitionSpec as P


AXES = ("by", "bx")
ITERS = 4
TILE = 8
REACH = 4
CENTER = 5.0
HALFWIDTH = 4.0
VMEM_GRANT = 12 << 20
LIMIT = 1000.0


def lanes_of(shape):
    return lax.broadcasted_iota(jnp.int32, shape, 1)


def rows_of(shape):
    return lax.broadcasted_iota(jnp.int32, shape, 0)


def roll(value, shift, axis=1):
    size = value.shape[axis]
    shift = shift % size
    return value if shift == 0 else pltpu.roll(value, shift, axis)


def grouped_sum(value, first, last):
    step = first
    while step < last:
        value = value + roll(value, step)
        step *= 2
    return value


def unfold(block, rows, levels):
    half = block[: rows // 2]
    return jnp.concatenate([half, roll(half, -(6 * levels + 16))], axis=0)


def level_terms(kmt, k, di, u, v):
    wet = kmt > k
    mixing = jnp.where(wet, di, 0.0)
    across = jnp.where(wet, 0.5 * u, 0.0)
    along = jnp.where(wet, 0.5 * v, 0.0)
    return wet, 1.0 - 4.0 * mixing, mixing - across, mixing + across, mixing - along, mixing + along


def within(value, own, c_east, c_west, c_north, c_south):
    return (
        value * own
        + c_east * roll(value, -1)
        + c_west * roll(value, 1)
        + c_north * roll(value, -1, 0)
        + c_south * roll(value, 1, 0)
    )


def inside(c_east, c_west, c_north, c_south, lane, row):
    rows, cols = lane.shape
    return (
        jnp.where(lane == cols - 1, 0.0, c_east),
        jnp.where(lane == 0, 0.0, c_west),
        jnp.where(row == rows - 1, 0.0, c_north),
        jnp.where(row == 0, 0.0, c_south),
    )


def stencil_kernel(
    tr_hbm, ve_hbm, di_hbm, kmt_hbm, fo_hbm, fs_hbm, packed, top, bottom, rhs_out, weight, tr, ve, di, kmt_ref, fs, fo, sems, flat_sems
):
    levels = tr.shape[1]
    rows, cols = kmt_ref.shape
    chunk = rows // 2
    flat = [
        pltpu.make_async_copy(source, target, flat_sems.at[i])
        for i, (source, target) in enumerate(((kmt_hbm, kmt_ref), (fs_hbm, fs), (fo_hbm, fo)))
    ]
    for copy in flat:
        copy.start()
    copies = []
    for c in range(rows // chunk):
        part = pl.ds(c * chunk, chunk)
        trio = (
            pltpu.make_async_copy(tr_hbm.at[:, :, part], tr.at[:, :, part], sems.at[c, 0]),
            pltpu.make_async_copy(ve_hbm.at[:, :, part], ve.at[:, :, part], sems.at[c, 1]),
            pltpu.make_async_copy(di_hbm.at[:, part], di.at[:, part], sems.at[c, 2]),
        )
        for copy in trio:
            copy.start()
        copies.append(trio)
    shape = (chunk, cols)
    lane, row = lanes_of(shape), rows_of(shape)
    base = 6 * levels
    first, last = lane == 0, lane == cols - 1
    lean = jnp.where(last, -0.5, 0.5)
    pack = jnp.zeros(shape, jnp.float32)
    for copy in flat:
        copy.wait()
    ready = 0
    for c in range(rows // chunk):
        start = c * chunk
        while ready < min(c + 2, rows // chunk):
            for copy in copies[ready]:
                copy.wait()
            ready += 1
        part = pl.ds(start, chunk)
        kmt = kmt_ref[part, :]
        offset = c * (6 * levels + 16)
        heavy = jnp.where(kmt > 0, 4.0 + fs[part, :], 0.0)
        weight[part, :] = heavy
        mixed = jnp.zeros(shape, jnp.float32)
        carried = jnp.zeros(shape, jnp.float32)

        def row_jump(k, at):
            if at < 0 or at >= rows:
                return jnp.zeros((1, cols), jnp.float32)
            one = pl.ds(at, 1)
            return jnp.where(kmt_ref[one, :] > k, tr[0, k, one, :] - tr[1, k, one, :], 0.0)

        for k in range(levels):
            wet = kmt > k
            values = [jnp.where(wet, tr[t, k, part, :], 0.0) for t in range(2)]
            mixing, u, v = di[k, part, :], ve[0, k, part, :], ve[1, k, part, :]
            edge = jnp.where(wet, mixing + lean * u, 0.0)
            for i, field in enumerate((*values, edge)):
                slot = offset // 2 + i * levels + k
                pack = jnp.where((lane // 2) == slot, roll(field, 2 * slot + 1), pack)
            jump = values[0] - values[1]
            east = jnp.where(last, 0.0, roll(jump, -1))
            west = jnp.where(first, 0.0, roll(jump, 1))
            north = jnp.where(row == chunk - 1, row_jump(k, start + chunk), roll(jump, -1, 0))
            south = jnp.where(row == 0, row_jump(k, start - 1), roll(jump, 1, 0))
            around = (east + west) + (north + south) - 4.0 * jump
            mixed = mixed + jnp.where(wet, jump + mixing * around, 0.0)
            carried = carried + jnp.where(wet, u * (east - west) + v * (north - south), 0.0)
            for ref, at, sign in ((bottom, 0, 0.5), (top, rows - 1, -0.5)):
                if start <= at < start + chunk:
                    here = slice(at - start, at - start + 1)
                    for i, field in enumerate(values):
                        ref[pl.ds(i * levels + k, 1), :] = field[here]
                    ref[pl.ds(2 * levels + k, 1), :] = jnp.where(wet[here], mixing[here] + sign * v[here], 0.0)
        rhs = jnp.where(kmt > 0, fo[part, :] + (mixed - 0.5 * carried) / levels, 0.0)
        rhs_out[part, :] = rhs
        for i, field in enumerate((rhs, heavy)):
            at = offset + base + 8 * i
            pack = jnp.where((lane // 8) == at // 8, roll(field, at + REACH), pack)
    packed[pl.ds(0, chunk), :] = pack
    small = (levels, cols)
    lane_s, row_s = lanes_of(small), rows_of(small)
    corner = jnp.zeros((TILE, cols), jnp.float32)
    row_c = rows_of((TILE, cols))
    for i, ref in enumerate((bottom, top)):
        jump = ref[pl.ds(0, levels), :] - ref[pl.ds(levels, levels), :]
        past = ref[pl.ds(2 * levels, levels), :]
        line = jnp.zeros(small, jnp.float32)
        for start, field in ((0, jump), (8 * levels, past)):
            spread = pltpu.roll(field, (start + REACH) % cols, 1, stride=8, stride_axis=0)
            line = line + jnp.where((lane_s // 8) == start // 8 + row_s, spread, 0.0)
        corner = jnp.where(row_c == i, jnp.sum(line, axis=0, keepdims=True), corner)
    packed[pl.ds(chunk, TILE), :] = corner


def tracers_kernel(tr, ve, di, kmt_ref, own_ref, east_west_a, east_west_b, top, bottom, north_south_a, north_south_b, new_out):
    levels = tr.shape[1]
    rows, cols = kmt_ref.shape
    shape = (rows, cols)
    lane, row = lanes_of(shape), rows_of(shape)
    kmt = kmt_ref[...]
    east, west = sides("bx", east_west_a[pl.ds(0, rows // 2), :], east_west_b[pl.ds(0, rows // 2), :])
    east, west = unfold(east, rows, levels), unfold(west, rows, levels)
    north, south = sides("by", north_south_a[pl.ds(0, 3 * levels), :], north_south_b[pl.ds(0, 3 * levels), :])
    beyond = jnp.where(lane % 2 == 0, roll(east, -1), roll(west, 1))
    mine = unfold(own_ref[pl.ds(0, rows // 2), :], rows, levels)
    ends = (lane == 0) | (lane == cols - 1)
    top_v, bottom_v = top[...], bottom[...]
    added = [mine * roll(beyond, 4 * levels - 2 * levels * t) for t in range(2)]
    above = [top_v[2 * levels :] * north[t * levels : (t + 1) * levels] for t in range(2)]
    below = [bottom_v[2 * levels :] * south[t * levels : (t + 1) * levels] for t in range(2)]
    for k in range(levels):
        wet, own, *around = level_terms(kmt, k, di[k], ve[0, k], ve[1, k])
        around = inside(*around, lane, row)
        for t in range(2):
            value = within(jnp.where(wet, tr[t, k], 0.0), own, *around)
            value = value + jnp.where(ends, roll(added[t], cols - 1 - (4 * levels + 2 * k)), 0.0)
            value = value + jnp.where(row == rows - 1, above[t][k : k + 1], 0.0) + jnp.where(row == 0, below[t][k : k + 1], 0.0)
            new_out[t, k] = value


def is_even(axis):
    return lax.axis_index(axis) % 2 == 0 if lax.axis_size(axis) % 2 == 0 else lax.axis_size(axis) > 0


def sides(axis, got_a, got_b):
    index, even = lax.axis_index(axis), is_even(axis)
    after = jnp.where(even, got_a, got_b)
    before = jnp.where(even, got_b, got_a)
    return jnp.where(index < lax.axis_size(axis) - 1, after, 0.0), jnp.where(index > 0, before, 0.0)


def columns_kernel(got_a, got_b, packed, top, bottom, weight, rhs_in, strip_out, rhs_out, send_a, send_b):
    rows, cols = weight.shape
    levels = top.shape[0] // 3
    east, west = sides("bx", got_a[...], got_b[...])
    shape = (rows, cols)
    lane = lanes_of(shape)
    mine = unfold(packed[pl.ds(0, rows // 2), :], rows, levels)
    e, w = unfold(east, rows, levels), unfold(west, rows, levels)
    beyond = jnp.where(lane % 2 == 0, roll(e, -1), roll(w, 1))
    jump_beyond = roll(beyond, 4 * levels) - roll(beyond, 2 * levels)
    jump_mine = roll(mine, 4 * levels) - roll(mine, 2 * levels)
    here = (lane >= 4 * levels) & (lane < 6 * levels)
    inward = jnp.where(here, mine * jump_beyond, 0.0)
    outward = jnp.where(here, beyond * jump_mine, 0.0)
    both = inward + roll(outward, 2 * levels)
    both = grouped_sum(both, 2, 2 * levels) / levels
    ends = (lane == 0) | (lane == cols - 1)
    rhs = rhs_in[...] + jnp.where(ends, roll(both, cols - 1 - (6 * levels - 2)), 0.0)
    rhs_out[...] = rhs
    base = 6 * levels
    first = roll(both, base + REACH - (8 * levels - 2))
    second = roll(both, base + REACH - 1 - (8 * levels - 1))
    body = jnp.where(lane % 8 < REACH, w, e) + jnp.where(lane == base + REACH, first, 0.0) + jnp.where(lane == base + REACH - 1, second, 0.0)
    strip_out[pl.ds(0, rows), :] = body
    tile = (TILE, cols)
    corner = jnp.where(lanes_of(tile) % 8 < REACH, west[rows // 2 :], east[rows // 2 :])
    strip_out[pl.ds(rows, TILE), :] = corner
    row = rows_of(tile)
    heavy = weight[...]
    n3 = 3 * levels
    above = (
        top[...],
        jnp.where(row < REACH, roll(heavy[rows - TILE :], REACH, 0), rhs[rows - TILE :]),
        jnp.where(row == 0, corner[1:2], body[rows - TILE :]),
    )
    below = (
        bottom[...],
        jnp.where(row < REACH, rhs[:TILE], roll(heavy[:TILE], REACH, 0)),
        jnp.where(row == REACH, corner[:1], body[:TILE]),
    )
    even = is_even("by")
    for ref, one, two in ((send_a, above, below), (send_b, below, above)):
        ref[pl.ds(0, n3), :] = jnp.where(even, one[0], two[0])
        ref[pl.ds(n3, TILE), :] = jnp.where(even, one[1], two[1])
        ref[pl.ds(n3 + TILE, TILE), :] = jnp.where(even, one[2], two[2])


def rows_kernel(got_a, got_b, top, bottom, weight, rhs_in, strip_in, basis, moments):
    rows, cols = weight.shape
    levels = top.shape[0] // 3
    north, south = sides("by", got_a[...], got_b[...])
    n3 = 3 * levels

    def jump(block):
        return block[:levels] - block[levels : 2 * levels]

    def dot(coefficient, value):
        return jnp.sum(coefficient * value, axis=0, keepdims=True) / levels

    top_v, bottom_v = top[...], bottom[...]
    add_top = dot(top_v[2 * levels :], jump(north[:n3]))
    add_bottom = dot(bottom_v[2 * levels :], jump(south[:n3]))
    add_north = dot(north[2 * levels : n3], jump(top_v))
    add_south = dot(south[2 * levels : n3], jump(bottom_v))
    corner = strip_in[pl.ds(rows, TILE), :]
    low, high = corner[:1], corner[1:2]
    c_north, c_south = north[n3 + TILE + REACH : n3 + TILE + REACH + 1], south[n3 + TILE : n3 + TILE + 1]
    half = 8 * levels
    edge = (1, cols)
    lane_1 = lanes_of(edge)

    def cross(coefficient, value):
        product = jnp.where(lane_1 >= half, coefficient * roll(value, half), 0.0)
        summed = grouped_sum(product, 8, 8 * levels) / levels
        return jnp.where((lane_1 // 8) == 6 * levels // 8, roll(summed, 6 * levels - (16 * levels - 8)), 0.0)

    strip_top, strip_bottom = cross(high, c_north), cross(low, c_south)
    strip_north, strip_south = cross(c_north, high), cross(c_south, low)

    extended = (rows + 2 * TILE, cols)
    row = rows_of(extended)
    lane = lanes_of(extended)

    outer = rows_of((TILE, cols))
    flat_n, flat_s = north[n3 : n3 + TILE], south[n3 : n3 + TILE]
    strip_n, strip_s = north[n3 + TILE :], south[n3 + TILE :]

    def extend(own, above, below):
        pieces = [own, jnp.where(outer < REACH, above, 0.0), jnp.where(outer >= TILE - REACH, below, 0.0)]
        return jnp.concatenate(pieces, axis=0)

    def patch(field, at_top, at_bottom, at_north, at_south):
        field = field + jnp.where(row == rows - 1, at_top, 0.0) + jnp.where(row == 0, at_bottom, 0.0)
        return field + jnp.where(row == rows, at_north, 0.0) + jnp.where(row == rows + 2 * TILE - 1, at_south, 0.0)

    rhs_c = patch(extend(rhs_in[...], flat_n, flat_s), add_top, add_bottom, add_north, add_south)
    heavy_c = extend(weight[...], roll(flat_n, REACH, 0), roll(flat_s, REACH, 0))
    strip = extend(strip_in[pl.ds(0, rows), :], strip_n, strip_s)
    strip = patch(strip, strip_top, strip_bottom, strip_north, strip_south)
    near = (lane < REACH) | (lane >= cols - REACH)
    base = 6 * levels
    rhs_s, heavy_s = (jnp.where(near, roll(strip, cols - REACH - base - 8 * i), 0.0) for i in range(2))

    scale = 1.0 / HALFWIDTH
    diag_c, side_c = jnp.where(heavy_c > 0, (heavy_c - CENTER) * scale, 0.0), jnp.where(heavy_c > 0, scale, 0.0)
    diag_s, side_s = jnp.where(heavy_s > 0, (heavy_s - CENTER) * scale, 0.0), jnp.where(heavy_s > 0, scale, 0.0)
    right, left = lane == cols - 1, lane == 0

    def apply(c, s):
        rc, rs, lc, ls = roll(c, -1), roll(s, -1), roll(c, 1), roll(s, 1)
        around_c = jnp.where(right, rs, rc) + jnp.where(left, ls, lc) + roll(c, -1, 0) + roll(c, 1, 0)
        around_s = jnp.where(right, rc, rs) + jnp.where(left, lc, ls) + roll(s, -1, 0) + roll(s, 1, 0)
        return diag_c * c - side_c * around_c, diag_s * s - side_s * around_s

    vectors = [(rhs_c, rhs_s)]
    vectors.append(apply(*vectors[0]))
    for _ in range(ITERS - 1):
        c, s = apply(*vectors[-1])
        vectors.append((2.0 * c - vectors[-2][0], 2.0 * s - vectors[-2][1]))
    inner = [c[:rows] for c, _ in vectors]
    line = jnp.zeros(edge, jnp.float32)
    at = 0
    for i in range(ITERS + 1):
        basis[i] = inner[i]
        for j in range(i, ITERS + 1):
            product = (inner[i] * inner[j]).reshape(rows // TILE, TILE, cols).sum(axis=0)
            whole = jnp.sum(jnp.sum(product, axis=0, keepdims=True), axis=1, keepdims=True)
            line = jnp.where(lane_1 == at, whole, line)
            at += 1
    moments[...] = jnp.broadcast_to(line[None], moments.shape)


def times(coefficients):
    out = [None] * (len(coefficients) + 1)

    def put(at, value):
        out[at] = value if out[at] is None else out[at] + value

    for j, c in enumerate(coefficients):
        put(j, CENTER * c)
        if j == 0:
            put(1, HALFWIDTH * c)
        else:
            put(j + 1, 0.5 * HALFWIDTH * c)
            put(j - 1, 0.5 * HALFWIDTH * c)
    return out


def mix(a, b, factor):
    out = []
    for j in range(max(len(a), len(b))):
        if j >= len(b):
            out.append(a[j])
        elif j >= len(a):
            out.append(factor * b[j])
        else:
            out.append(a[j] + factor * b[j])
    return out


def solve_kernel(got, basis, surface_out, residual_out, flag, results, sems):
    size = ITERS + 1
    line = jnp.sum(got[...], axis=0)
    lane_1 = lanes_of(line.shape)
    gram, at = {}, 0
    for i in range(size):
        for j in range(i, size):
            gram[i, j] = gram[j, i] = jnp.sum(jnp.where(lane_1 == at, line, 0.0), axis=1, keepdims=True)
            at += 1

    def inner(a, b):
        exact = bound = None
        for i, x in enumerate(a):
            for j, y in enumerate(b):
                term = x * y * gram[i, j]
                exact = term if exact is None else exact + term
                bound = jnp.abs(term) if bound is None else bound + jnp.abs(term)
        return exact, bound

    one = jnp.ones_like(gram[0, 0])
    good = one > 0
    residual = [one]
    image = times(residual)
    now, _ = inner(residual, residual)
    product, _ = inner(residual, image)
    alpha = now / product
    direction, along = residual, image
    surface = []
    for step in range(ITERS):
        surface = mix(surface, direction, alpha)
        residual = mix(residual, along, -alpha)
        if step + 1 < ITERS:
            image = times(residual)
            following, bound = inner(residual, residual)
            good = good & (bound <= LIMIT * following)
            product, bound = inner(residual, image)
            good = good & (bound <= LIMIT * product)
            ratio = following / now
            taken = ratio * following / alpha
            good = good & (product + taken <= 0.1 * LIMIT * (product - taken))
            alpha = following / (product - taken)
            direction = mix(residual, direction, ratio)
            along = mix(image, along, ratio)
            now = following
    last, _ = inner(residual, residual)
    good = good & (now <= 0.1 * LIMIT * last)
    vectors = [basis[i] for i in range(size)]
    copies = []
    for at, (ref, combination) in enumerate(((surface_out, surface), (residual_out, residual))):
        total = combination[0] * vectors[0]
        for j in range(1, len(combination)):
            total = total + combination[j] * vectors[j]
        results[at] = total
        copies.append(pltpu.make_async_copy(results.at[at], ref, sems.at[at]))
        copies[at].start()
    flag[0, 0] = jnp.where(good, 1, 0)[0, 0]
    for copy in copies:
        copy.wait()


def linear(axis, index, other):
    row, column = (index, other) if axis == AXES[0] else (other, index)
    return row * lax.axis_size(AXES[1]) + column


def exchange(first, second, axis):
    peers = lax.axis_size(axis)
    if peers % 2:
        up = [(i, i + 1) for i in range(peers - 1)]
        down = [(j, i) for i, j in up]
        return lax.ppermute(second, axis, down), lax.ppermute(first, axis, up)
    pairs_a = [(i, i ^ 1) for i in range(peers)]
    pairs_b = [(i, (i + 1) % peers if i % 2 else (i - 1) % peers) for i in range(peers)]
    other, = [name for name in AXES if name != axis]
    if lax.axis_size(other) % 2 == 0:
        far = []
        for i in range(peers):
            for j in range(lax.axis_size(other)):
                target = (i, j ^ 1) if i in (0, peers - 1) else (pairs_b[i][1], j)
                far.append((linear(axis, i, j), linear(axis, *target)))
        axes, pairs_b = AXES, far
    else:
        axes = axis
    got_a = lax.ppermute(first, axis, pairs_a)
    got_b = lax.ppermute(second, axes, pairs_b)
    return got_a, got_b


def padded_2(value, axes, width):
    for axis, dim in axes:
        peers, length = (lax.axis_size(axis), value.shape[dim])
        up = [(i, (i + 1) % peers) for i in range(peers - 1)]
        down = [(j, i) for i, j in up]
        last = lax.slice_in_dim(value, length - width, length, axis=dim)
        first = lax.slice_in_dim(value, 0, width, axis=dim)
        before = lax.ppermute(last, axis, up)
        after = lax.ppermute(first, axis, down)
        value = jnp.concatenate([before, value, after], axis=dim)
    return value


def step_by_step(rhs, kmt, free_surface):
    ocean = (kmt > 0).astype(jnp.float32)
    weight = ocean * (4.0 + free_surface)

    def operate(field):
        padded = padded_2(field, (("by", 0), ("bx", 1)), 1)
        around = padded[1:-1, 2:] + padded[1:-1, :-2] + padded[2:, 1:-1] + padded[:-2, 1:-1]
        return weight * field - ocean * around

    def pair(a, b):
        return lax.psum(lax.psum((jnp.sum(a * a), jnp.sum(a * b)), "bx"), "by")

    surface, residual = jnp.zeros_like(rhs), rhs
    image = operate(residual)
    now, product = pair(residual, image)
    alpha = now / product
    direction, along = residual, image
    for step in range(ITERS):
        surface = surface + alpha * direction
        residual = residual - alpha * along
        if step + 1 < ITERS:
            image = operate(residual)
            following, product = pair(residual, image)
            ratio = following / now
            alpha = following / (product - ratio * following / alpha)
            direction = residual + ratio * direction
            along = image + ratio * along
            now = following
    return surface, residual


def call(kernel, out_shape, kinds, out_kinds=None, scratch=(), cost=None, resident=True):
    spaces = {"s": pltpu.SMEM, "v": pltpu.VMEM, "h": pltpu.HBM}
    out_kinds = out_kinds or "v" * len(out_shape)
    if resident:
        out_shape = [spaces[k](o.shape, o.dtype) for k, o in zip(out_kinds, out_shape)]
    return pl.pallas_call(
        kernel,
        out_shape=out_shape,
        in_specs=[pl.BlockSpec(memory_space=spaces[k]) for k in kinds],
        out_specs=[pl.BlockSpec(memory_space=spaces[k]) for k in out_kinds],
        scratch_shapes=scratch,
        cost_estimate=cost,
        compiler_params=pltpu.CompilerParams(vmem_limit_bytes=VMEM_GRANT),
    )


def f32(*shape):
    return jax.ShapeDtypeStruct(shape, jnp.float32)


def per_device(*inputs):
    tracers, kmt = inputs[0], inputs[3]
    levels = tracers.shape[1]
    rows, cols = kmt.shape
    everyone = lax.axis_size("by") * lax.axis_size("bx")
    lines = 3 * levels
    packed, top, bottom, rhs, weight, tracers, velocity, diffusivity, kmt = call(
        stencil_kernel,
        [f32(rows // 2 + TILE, cols), f32(lines, cols), f32(lines, cols), f32(rows, cols), f32(rows, cols)]
        + [jax.ShapeDtypeStruct(v.shape, v.dtype) for v in inputs[:4]],
        "h" * 6,
        scratch=[
            pltpu.VMEM((rows, cols), jnp.float32),
            pltpu.VMEM((rows, cols), jnp.float32),
            pltpu.SemaphoreType.DMA((2, 3)),
            pltpu.SemaphoreType.DMA((3,)),
        ],
    )(*[pltpu.with_memory_space_constraint(v, pltpu.HBM) for v in inputs])
    x_a, x_b = exchange(packed, packed, "bx")
    deep = lines + 2 * TILE
    strip, rhs, send_a, send_b = call(
        columns_kernel,
        [f32(rows + TILE, cols), f32(rows, cols), f32(deep, cols), f32(deep, cols)],
        "v" * 7,
    )(x_a, x_b, packed, top, bottom, weight, rhs)
    y_a, y_b = exchange(send_a, send_b, "by")
    basis, moments = call(
        rows_kernel,
        [f32(ITERS + 1, rows, cols), f32(everyone, 1, cols)],
        "v" * 7,
    )(y_a, y_b, top, bottom, weight, rhs, strip)
    got = lax.all_to_all(moments, ("by", "bx"), 0, 0, tiled=True)
    new_tracers, = call(
        tracers_kernel,
        [f32(*tracers.shape)],
        "v" * 11,
        resident=False,
        cost=pl.CostEstimate(flops=30 * tracers.size, bytes_accessed=16 * tracers.size, transcendentals=0),
    )(tracers, velocity, diffusivity, kmt, packed, x_a, x_b, top, bottom, y_a, y_b)
    surface, residual, flag = call(
        solve_kernel,
        [f32(rows, cols), f32(rows, cols), jax.ShapeDtypeStruct((1, 1), jnp.int32)],
        "vv",
        "hhs",
        scratch=[pltpu.VMEM((2, rows, cols), jnp.float32), pltpu.SemaphoreType.DMA((2,))],
    )(got, basis)
    surface, residual = lax.cond(
        flag[0, 0] == 1,
        lambda: (surface, residual),
        lambda: step_by_step(basis[0], inputs[3], inputs[5]),
    )
    return new_tracers, surface, residual


def solution(mesh):
    placed = (
        P(None, None, "by", "bx"),
        P(None, None, "by", "bx"),
        P(None, "by", "bx"),
        P("by", "bx"),
        P("by", "bx"),
        P("by", "bx"),
    )
    return jax.shard_map(
        per_device,
        mesh=mesh,
        in_specs=placed,
        out_specs=(P(None, None, "by", "bx"), P("by", "bx"), P("by", "bx")),
        check_vma=False,
    )
```

```python
import jax
import jax.numpy as jnp
from jax import lax
from jax.experimental import pallas as pl
from jax.experimental.pallas import tpu as pltpu
from jax.sharding import PartitionSpec as P


AXES = ("by", "bx")
ITERS = 4
TILE = 8
REACH = 4
CENTER = 5.0
HALFWIDTH = 4.0
VMEM_GRANT = 12 << 20
GROUPS = 2
LIMIT = 1000.0


def lanes_of(shape):
    return lax.broadcasted_iota(jnp.int32, shape, 1)


def rows_of(shape):
    return lax.broadcasted_iota(jnp.int32, shape, 0)


def roll(value, shift, axis=1):
    size = value.shape[axis]
    shift = shift % size
    return value if shift == 0 else pltpu.roll(value, shift, axis)


def grouped_sum(value, first, last):
    step = first
    while step < last:
        value = value + roll(value, step)
        step *= 2
    return value


def unfold(block, rows, levels):
    half = block[: rows // 2]
    return jnp.concatenate([half, roll(half, -(6 * levels + 16))], axis=0)


def level_terms(kmt, k, di, u, v):
    wet = kmt > k
    mixing = jnp.where(wet, di, 0.0)
    across = jnp.where(wet, 0.5 * u, 0.0)
    along = jnp.where(wet, 0.5 * v, 0.0)
    return wet, 1.0 - 4.0 * mixing, mixing - across, mixing + across, mixing - along, mixing + along


def within(value, own, c_east, c_west, c_north, c_south):
    return (
        value * own
        + c_east * roll(value, -1)
        + c_west * roll(value, 1)
        + c_north * roll(value, -1, 0)
        + c_south * roll(value, 1, 0)
    )


def inside(c_east, c_west, c_north, c_south, lane, row):
    rows, cols = lane.shape
    return (
        jnp.where(lane == cols - 1, 0.0, c_east),
        jnp.where(lane == 0, 0.0, c_west),
        jnp.where(row == rows - 1, 0.0, c_north),
        jnp.where(row == 0, 0.0, c_south),
    )


def stencil_kernel(
    tr_hbm, ve_hbm, di_hbm, kmt_hbm, fo_hbm, fs_hbm, packed, top, bottom, rhs_out, weight, tr, ve, di, kmt_ref, fs, fo, sems, flat_sems
):
    levels = tr.shape[1]
    rows, cols = kmt_ref.shape
    chunk = rows // 2
    flat = [
        pltpu.make_async_copy(source, target, flat_sems.at[i])
        for i, (source, target) in enumerate(((kmt_hbm, kmt_ref), (fs_hbm, fs), (fo_hbm, fo)))
    ]
    for copy in flat:
        copy.start()
    span = levels // GROUPS
    copies = []
    for c, (begin, length) in enumerate(((0, chunk + TILE), (chunk + TILE, chunk - TILE))):
        part = pl.ds(begin, length)
        for g in range(GROUPS):
            deep = pl.ds(g * span, span)
            trio = (
                pltpu.make_async_copy(tr_hbm.at[:, deep, part], tr.at[:, deep, part], sems.at[c, g, 0]),
                pltpu.make_async_copy(ve_hbm.at[:, deep, part], ve.at[:, deep, part], sems.at[c, g, 1]),
                pltpu.make_async_copy(di_hbm.at[deep, part], di.at[deep, part], sems.at[c, g, 2]),
            )
            for copy in trio:
                copy.start()
            copies.append(trio)
    shape = (chunk, cols)
    lane, row = lanes_of(shape), rows_of(shape)
    base = 6 * levels
    first, last = lane == 0, lane == cols - 1
    lean = jnp.where(last, -0.5, 0.5)
    pack = jnp.zeros(shape, jnp.float32)
    for copy in flat:
        copy.wait()
    for c in range(rows // chunk):
        start = c * chunk
        part = pl.ds(start, chunk)
        kmt = kmt_ref[part, :]
        offset = c * (6 * levels + 16)
        heavy = jnp.where(kmt > 0, 4.0 + fs[part, :], 0.0)
        weight[part, :] = heavy
        mixed = jnp.zeros(shape, jnp.float32)
        carried = jnp.zeros(shape, jnp.float32)

        def row_jump(k, at):
            if at < 0 or at >= rows:
                return jnp.zeros((1, cols), jnp.float32)
            one = pl.ds(at, 1)
            return jnp.where(kmt_ref[one, :] > k, tr[0, k, one, :] - tr[1, k, one, :], 0.0)

        for k in range(levels):
            if k % span == 0:
                for copy in copies[c * GROUPS + k // span]:
                    copy.wait()
            wet = kmt > k
            values = [jnp.where(wet, tr[t, k, part, :], 0.0) for t in range(2)]
            mixing, u, v = di[k, part, :], ve[0, k, part, :], ve[1, k, part, :]
            edge = jnp.where(wet, mixing + lean * u, 0.0)
            for i, field in enumerate((*values, edge)):
                slot = offset // 2 + i * levels + k
                pack = jnp.where((lane // 2) == slot, roll(field, 2 * slot + 1), pack)
            jump = values[0] - values[1]
            east = jnp.where(last, 0.0, roll(jump, -1))
            west = jnp.where(first, 0.0, roll(jump, 1))
            north = jnp.where(row == chunk - 1, row_jump(k, start + chunk), roll(jump, -1, 0))
            south = jnp.where(row == 0, row_jump(k, start - 1), roll(jump, 1, 0))
            around = (east + west) + (north + south) - 4.0 * jump
            mixed = mixed + jnp.where(wet, jump + mixing * around, 0.0)
            carried = carried + jnp.where(wet, u * (east - west) + v * (north - south), 0.0)
            for ref, at, sign in ((bottom, 0, 0.5), (top, rows - 1, -0.5)):
                if start <= at < start + chunk:
                    here = slice(at - start, at - start + 1)
                    for i, field in enumerate(values):
                        ref[pl.ds(i * levels + k, 1), :] = field[here]
                    ref[pl.ds(2 * levels + k, 1), :] = jnp.where(wet[here], mixing[here] + sign * v[here], 0.0)
        rhs = jnp.where(kmt > 0, fo[part, :] + (mixed - 0.5 * carried) / levels, 0.0)
        rhs_out[part, :] = rhs
        for i, field in enumerate((rhs, heavy)):
            at = offset + base + 8 * i
            pack = jnp.where((lane // 8) == at // 8, roll(field, at + REACH), pack)
    packed[pl.ds(0, chunk), :] = pack
    small = (levels, cols)
    lane_s, row_s = lanes_of(small), rows_of(small)
    corner = jnp.zeros((TILE, cols), jnp.float32)
    row_c = rows_of((TILE, cols))
    for i, ref in enumerate((bottom, top)):
        jump = ref[pl.ds(0, levels), :] - ref[pl.ds(levels, levels), :]
        past = ref[pl.ds(2 * levels, levels), :]
        line = jnp.zeros(small, jnp.float32)
        for start, field in ((0, jump), (8 * levels, past)):
            spread = pltpu.roll(field, (start + REACH) % cols, 1, stride=8, stride_axis=0)
            line = line + jnp.where((lane_s // 8) == start // 8 + row_s, spread, 0.0)
        corner = jnp.where(row_c == i, jnp.sum(line, axis=0, keepdims=True), corner)
    packed[pl.ds(chunk, TILE), :] = corner


def tracers_kernel(tr, ve, di, kmt_ref, own_ref, east_west_a, east_west_b, top, bottom, north_south_a, north_south_b, new_out):
    levels = tr.shape[1]
    rows, cols = kmt_ref.shape
    shape = (rows, cols)
    lane, row = lanes_of(shape), rows_of(shape)
    kmt = kmt_ref[...]
    east, west = sides("bx", east_west_a[pl.ds(0, rows // 2), :], east_west_b[pl.ds(0, rows // 2), :])
    east, west = unfold(east, rows, levels), unfold(west, rows, levels)
    north, south = sides("by", north_south_a[pl.ds(0, 3 * levels), :], north_south_b[pl.ds(0, 3 * levels), :])
    beyond = jnp.where(lane % 2 == 0, roll(east, -1), roll(west, 1))
    mine = unfold(own_ref[pl.ds(0, rows // 2), :], rows, levels)
    ends = (lane == 0) | (lane == cols - 1)
    top_v, bottom_v = top[...], bottom[...]
    added = [mine * roll(beyond, 4 * levels - 2 * levels * t) for t in range(2)]
    above = [top_v[2 * levels :] * north[t * levels : (t + 1) * levels] for t in range(2)]
    below = [bottom_v[2 * levels :] * south[t * levels : (t + 1) * levels] for t in range(2)]
    for k in range(levels):
        wet, own, *around = level_terms(kmt, k, di[k], ve[0, k], ve[1, k])
        around = inside(*around, lane, row)
        for t in range(2):
            value = within(jnp.where(wet, tr[t, k], 0.0), own, *around)
            value = value + jnp.where(ends, roll(added[t], cols - 1 - (4 * levels + 2 * k)), 0.0)
            value = value + jnp.where(row == rows - 1, above[t][k : k + 1], 0.0) + jnp.where(row == 0, below[t][k : k + 1], 0.0)
            new_out[t, k] = value


def is_even(axis):
    return lax.axis_index(axis) % 2 == 0 if lax.axis_size(axis) % 2 == 0 else lax.axis_size(axis) > 0


def sides(axis, got_a, got_b):
    index, even = lax.axis_index(axis), is_even(axis)
    after = jnp.where(even, got_a, got_b)
    before = jnp.where(even, got_b, got_a)
    return jnp.where(index < lax.axis_size(axis) - 1, after, 0.0), jnp.where(index > 0, before, 0.0)


def complete(mine, e, w, rhs, levels):
    cols = mine.shape[1]
    lane = lanes_of(mine.shape)
    beyond = jnp.where(lane % 2 == 0, roll(e, -1), roll(w, 1))
    jump_beyond = roll(beyond, 4 * levels) - roll(beyond, 2 * levels)
    jump_mine = roll(mine, 4 * levels) - roll(mine, 2 * levels)
    here = (lane >= 4 * levels) & (lane < 6 * levels)
    inward = jnp.where(here, mine * jump_beyond, 0.0)
    outward = jnp.where(here, beyond * jump_mine, 0.0)
    both = inward + roll(outward, 2 * levels)
    both = grouped_sum(both, 2, 2 * levels) / levels
    ends = (lane == 0) | (lane == cols - 1)
    rhs = rhs + jnp.where(ends, roll(both, cols - 1 - (6 * levels - 2)), 0.0)
    base = 6 * levels
    first = roll(both, base + REACH - (8 * levels - 2))
    second = roll(both, base + REACH - 1 - (8 * levels - 1))
    strip = jnp.where(lane % 8 < REACH, w, e)
    strip = strip + jnp.where(lane == base + REACH, first, 0.0) + jnp.where(lane == base + REACH - 1, second, 0.0)
    return rhs, strip


def ends_kernel(got_a, got_b, packed, top, bottom, weight, rhs_in, send_a, send_b, corner_out):
    rows, cols = weight.shape
    levels = top.shape[0] // 3
    east, west = sides("bx", got_a[...], got_b[...])

    def outer_rows(block):
        last = block[rows // 2 - TILE : rows // 2]
        return jnp.concatenate([block[:TILE], roll(last, -(6 * levels + 16))], axis=0)

    rhs = jnp.concatenate([rhs_in[pl.ds(0, TILE), :], rhs_in[pl.ds(rows - TILE, TILE), :]], axis=0)
    rhs, strip = complete(outer_rows(packed[...]), outer_rows(east), outer_rows(west), rhs, levels)
    tile = (TILE, cols)
    corner = jnp.where(lanes_of(tile) % 8 < REACH, west[rows // 2 :], east[rows // 2 :])
    corner_out[...] = corner
    row = rows_of(tile)
    first, last = weight[pl.ds(0, TILE), :], weight[pl.ds(rows - TILE, TILE), :]
    n3 = 3 * levels
    above = (
        top[...],
        jnp.where(row < REACH, roll(last, REACH, 0), rhs[TILE:]),
        jnp.where(row == 0, corner[1:2], strip[TILE:]),
    )
    below = (
        bottom[...],
        jnp.where(row < REACH, rhs[:TILE], roll(first, REACH, 0)),
        jnp.where(row == REACH, corner[:1], strip[:TILE]),
    )
    even = is_even("by")
    for ref, one, two in ((send_a, above, below), (send_b, below, above)):
        ref[pl.ds(0, n3), :] = jnp.where(even, one[0], two[0])
        ref[pl.ds(n3, TILE), :] = jnp.where(even, one[1], two[1])
        ref[pl.ds(n3 + TILE, TILE), :] = jnp.where(even, one[2], two[2])


def krylov(rhs_c, heavy_c, strip, heavy_strip):
    lane = lanes_of(rhs_c.shape)
    cols = rhs_c.shape[1]
    near = (lane < REACH) | (lane >= cols - REACH)
    rhs_s, heavy_s = jnp.where(near, strip, 0.0), jnp.where(near, heavy_strip, 0.0)
    scale = 1.0 / HALFWIDTH
    diag_c, side_c = jnp.where(heavy_c > 0, (heavy_c - CENTER) * scale, 0.0), jnp.where(heavy_c > 0, scale, 0.0)
    diag_s, side_s = jnp.where(heavy_s > 0, (heavy_s - CENTER) * scale, 0.0), jnp.where(heavy_s > 0, scale, 0.0)
    right, left = lane == cols - 1, lane == 0

    def apply(c, s):
        rc, rs, lc, ls = roll(c, -1), roll(s, -1), roll(c, 1), roll(s, 1)
        around_c = jnp.where(right, rs, rc) + jnp.where(left, ls, lc) + roll(c, -1, 0) + roll(c, 1, 0)
        around_s = jnp.where(right, rc, rs) + jnp.where(left, lc, ls) + roll(s, -1, 0) + roll(s, 1, 0)
        return diag_c * c - side_c * around_c, diag_s * s - side_s * around_s

    vectors = [(rhs_c, rhs_s)]
    vectors.append(apply(*vectors[0]))
    for _ in range(ITERS - 1):
        c, s = apply(*vectors[-1])
        vectors.append((2.0 * c - vectors[-2][0], 2.0 * s - vectors[-2][1]))
    return [c for c, _ in vectors]


def products(vectors):
    cols = vectors[0].shape[1]
    return [
        (vectors[i] * vectors[j]).reshape(-1, TILE, cols).sum(axis=0)
        for i in range(len(vectors))
        for j in range(i, len(vectors))
    ]


def spread(strip, levels):
    at = strip.shape[1] - REACH - 6 * levels
    return roll(strip, at), roll(strip, at - 8)


def middle_kernel(got_a, got_b, packed, top, weight, rhs_in, rhs_out, strip_out, basis, sums):
    rows, _ = weight.shape
    levels = top.shape[0] // 3
    east, west = sides("bx", got_a[pl.ds(0, rows // 2), :], got_b[pl.ds(0, rows // 2), :])
    mine = packed[pl.ds(0, rows // 2), :]
    rhs, strip = complete(*(unfold(v, rows, levels) for v in (mine, east, west)), rhs_in[...], levels)
    rhs_out[...] = rhs
    strip_out[...] = strip
    vectors = [v[TILE : rows - TILE] for v in krylov(rhs, weight[...], *spread(strip, levels))]
    for i, v in enumerate(vectors):
        basis[i] = v
    for i, v in enumerate(products(vectors)):
        sums[i] = v


def rows_kernel(got_a, got_b, top, bottom, weight, rhs_in, strip_in, corner_in, sums, basis, moments):
    rows, cols = weight.shape
    levels = top.shape[0] // 3
    north, south = sides("by", got_a[...], got_b[...])
    n3 = 3 * levels

    def jump(block):
        return block[:levels] - block[levels : 2 * levels]

    def dot(coefficient, value):
        return jnp.sum(coefficient * value, axis=0, keepdims=True) / levels

    top_v, bottom_v = top[...], bottom[...]
    add_top = dot(top_v[2 * levels :], jump(north[:n3]))
    add_bottom = dot(bottom_v[2 * levels :], jump(south[:n3]))
    add_north = dot(north[2 * levels : n3], jump(top_v))
    add_south = dot(south[2 * levels : n3], jump(bottom_v))
    corner = corner_in[...]
    low, high = corner[:1], corner[1:2]
    c_north, c_south = north[n3 + TILE + REACH : n3 + TILE + REACH + 1], south[n3 + TILE : n3 + TILE + 1]
    half = 8 * levels
    edge = (1, cols)
    lane_1 = lanes_of(edge)

    def cross(coefficient, value):
        product = jnp.where(lane_1 >= half, coefficient * roll(value, half), 0.0)
        summed = grouped_sum(product, 8, 8 * levels) / levels
        return jnp.where((lane_1 // 8) == 6 * levels // 8, roll(summed, 6 * levels - (16 * levels - 8)), 0.0)

    strip_top, strip_bottom = cross(high, c_north), cross(low, c_south)
    strip_north, strip_south = cross(c_north, high), cross(c_south, low)
    outer = rows_of((TILE, cols))
    flat_n, flat_s = north[n3 : n3 + TILE], south[n3 : n3 + TILE]

    def bands(ref, below, above):
        pieces = [jnp.where(outer >= TILE - REACH, below, 0.0), ref[pl.ds(0, 2 * TILE), :]]
        pieces += [ref[pl.ds(rows - 2 * TILE, 2 * TILE), :], jnp.where(outer < REACH, above, 0.0)]
        return jnp.concatenate(pieces, axis=0)

    row = rows_of((6 * TILE, cols))

    def patch(field, at_south, at_bottom, at_top, at_north):
        field = field + jnp.where(row == TILE - 1, at_south, 0.0) + jnp.where(row == TILE, at_bottom, 0.0)
        return field + jnp.where(row == 5 * TILE - 1, at_top, 0.0) + jnp.where(row == 5 * TILE, at_north, 0.0)

    rhs_c = patch(bands(rhs_in, flat_s, flat_n), add_south, add_bottom, add_top, add_north)
    heavy_c = bands(weight, roll(flat_s, REACH, 0), roll(flat_n, REACH, 0))
    strip = bands(strip_in, south[n3 + TILE :], north[n3 + TILE :])
    strip = patch(strip, strip_south, strip_bottom, strip_top, strip_north)
    vectors = krylov(rhs_c, heavy_c, *spread(strip, levels))
    vectors = [jnp.concatenate([v[TILE : 2 * TILE], v[4 * TILE : 5 * TILE]], axis=0) for v in vectors]
    line = jnp.zeros(edge, jnp.float32)
    for i, v in enumerate(vectors):
        basis[i] = v
    for i, v in enumerate(products(vectors)):
        whole = jnp.sum(jnp.sum(v + sums[i], axis=0, keepdims=True), axis=1, keepdims=True)
        line = jnp.where(lane_1 == i, whole, line)
    moments[...] = jnp.broadcast_to(line[None], moments.shape)


def times(coefficients):
    out = [None] * (len(coefficients) + 1)

    def put(at, value):
        out[at] = value if out[at] is None else out[at] + value

    for j, c in enumerate(coefficients):
        put(j, CENTER * c)
        if j == 0:
            put(1, HALFWIDTH * c)
        else:
            put(j + 1, 0.5 * HALFWIDTH * c)
            put(j - 1, 0.5 * HALFWIDTH * c)
    return out


def mix(a, b, factor):
    out = []
    for j in range(max(len(a), len(b))):
        if j >= len(b):
            out.append(a[j])
        elif j >= len(a):
            out.append(factor * b[j])
        else:
            out.append(a[j] + factor * b[j])
    return out


def solve_kernel(got, middle, outer, surface_out, residual_out, flag, results, sems):
    size = ITERS + 1
    line = jnp.sum(got[...], axis=0)
    lane_1 = lanes_of(line.shape)
    gram, at = {}, 0
    for i in range(size):
        for j in range(i, size):
            gram[i, j] = gram[j, i] = jnp.sum(jnp.where(lane_1 == at, line, 0.0), axis=1, keepdims=True)
            at += 1

    def inner(a, b):
        exact = bound = None
        for i, x in enumerate(a):
            for j, y in enumerate(b):
                term = x * y * gram[i, j]
                exact = term if exact is None else exact + term
                bound = jnp.abs(term) if bound is None else bound + jnp.abs(term)
        return exact, bound

    one = jnp.ones_like(gram[0, 0])
    good = one > 0
    residual = [one]
    image = times(residual)
    now, _ = inner(residual, residual)
    product, _ = inner(residual, image)
    alpha = now / product
    direction, along = residual, image
    surface = []
    for step in range(ITERS):
        surface = mix(surface, direction, alpha)
        residual = mix(residual, along, -alpha)
        if step + 1 < ITERS:
            image = times(residual)
            following, bound = inner(residual, residual)
            good = good & (bound <= LIMIT * following)
            product, bound = inner(residual, image)
            good = good & (bound <= LIMIT * product)
            ratio = following / now
            taken = ratio * following / alpha
            good = good & (product + taken <= 0.1 * LIMIT * (product - taken))
            alpha = following / (product - taken)
            direction = mix(residual, direction, ratio)
            along = mix(image, along, ratio)
            now = following
    last, _ = inner(residual, residual)
    good = good & (now <= 0.1 * LIMIT * last)
    rows = surface_out.shape[0]
    copies = []
    for at, (ref, combination) in enumerate(((surface_out, surface), (residual_out, residual))):
        for part, first, last in ((middle, TILE, rows - TILE), (outer, 0, 2 * TILE)):
            total = combination[0] * part[0]
            for j in range(1, len(combination)):
                total = total + combination[j] * part[j]
            if part is middle:
                results[at, pl.ds(first, last - first), :] = total
            else:
                results[at, pl.ds(0, TILE), :] = total[:TILE]
                results[at, pl.ds(rows - TILE, TILE), :] = total[TILE:]
        copies.append(pltpu.make_async_copy(results.at[at], ref, sems.at[at]))
        copies[at].start()
    flag[0, 0] = jnp.where(good, 1, 0)[0, 0]
    for copy in copies:
        copy.wait()


def linear(axis, index, other):
    row, column = (index, other) if axis == AXES[0] else (other, index)
    return row * lax.axis_size(AXES[1]) + column


def exchange(first, second, axis):
    peers = lax.axis_size(axis)
    if peers % 2:
        up = [(i, i + 1) for i in range(peers - 1)]
        down = [(j, i) for i, j in up]
        return lax.ppermute(second, axis, down), lax.ppermute(first, axis, up)
    pairs_a = [(i, i ^ 1) for i in range(peers)]
    pairs_b = [(i, (i + 1) % peers if i % 2 else (i - 1) % peers) for i in range(peers)]
    other, = [name for name in AXES if name != axis]
    if lax.axis_size(other) % 2 == 0:
        far = []
        for i in range(peers):
            for j in range(lax.axis_size(other)):
                target = (i, j ^ 1) if i in (0, peers - 1) else (pairs_b[i][1], j)
                far.append((linear(axis, i, j), linear(axis, *target)))
        axes, pairs_b = AXES, far
    else:
        axes = axis
    got_a = lax.ppermute(first, axis, pairs_a)
    got_b = lax.ppermute(second, axes, pairs_b)
    return got_a, got_b


def padded_2(value, axes, width):
    for axis, dim in axes:
        peers, length = (lax.axis_size(axis), value.shape[dim])
        up = [(i, (i + 1) % peers) for i in range(peers - 1)]
        down = [(j, i) for i, j in up]
        last = lax.slice_in_dim(value, length - width, length, axis=dim)
        first = lax.slice_in_dim(value, 0, width, axis=dim)
        before = lax.ppermute(last, axis, up)
        after = lax.ppermute(first, axis, down)
        value = jnp.concatenate([before, value, after], axis=dim)
    return value


def step_by_step(rhs, kmt, free_surface):
    ocean = (kmt > 0).astype(jnp.float32)
    weight = ocean * (4.0 + free_surface)

    def operate(field):
        padded = padded_2(field, (("by", 0), ("bx", 1)), 1)
        around = padded[1:-1, 2:] + padded[1:-1, :-2] + padded[2:, 1:-1] + padded[:-2, 1:-1]
        return weight * field - ocean * around

    def pair(a, b):
        return lax.psum(lax.psum((jnp.sum(a * a), jnp.sum(a * b)), "bx"), "by")

    surface, residual = jnp.zeros_like(rhs), rhs
    image = operate(residual)
    now, product = pair(residual, image)
    alpha = now / product
    direction, along = residual, image
    for step in range(ITERS):
        surface = surface + alpha * direction
        residual = residual - alpha * along
        if step + 1 < ITERS:
            image = operate(residual)
            following, product = pair(residual, image)
            ratio = following / now
            alpha = following / (product - ratio * following / alpha)
            direction = residual + ratio * direction
            along = image + ratio * along
            now = following
    return surface, residual


def call(kernel, out_shape, kinds, out_kinds=None, scratch=(), cost=None, resident=True):
    spaces = {"s": pltpu.SMEM, "v": pltpu.VMEM, "h": pltpu.HBM}
    out_kinds = out_kinds or "v" * len(out_shape)
    if resident:
        out_shape = [spaces[k](o.shape, o.dtype) for k, o in zip(out_kinds, out_shape)]
    return pl.pallas_call(
        kernel,
        out_shape=out_shape,
        in_specs=[pl.BlockSpec(memory_space=spaces[k]) for k in kinds],
        out_specs=[pl.BlockSpec(memory_space=spaces[k]) for k in out_kinds],
        scratch_shapes=scratch,
        cost_estimate=cost,
        compiler_params=pltpu.CompilerParams(vmem_limit_bytes=VMEM_GRANT),
    )


def f32(*shape):
    return jax.ShapeDtypeStruct(shape, jnp.float32)


def per_device(*inputs):
    tracers, kmt = inputs[0], inputs[3]
    levels = tracers.shape[1]
    rows, cols = kmt.shape
    everyone = lax.axis_size("by") * lax.axis_size("bx")
    lines = 3 * levels
    packed, top, bottom, rhs, weight, tracers, velocity, diffusivity, kmt = call(
        stencil_kernel,
        [f32(rows // 2 + TILE, cols), f32(lines, cols), f32(lines, cols), f32(rows, cols), f32(rows, cols)]
        + [jax.ShapeDtypeStruct(v.shape, v.dtype) for v in inputs[:4]],
        "h" * 6,
        scratch=[
            pltpu.VMEM((rows, cols), jnp.float32),
            pltpu.VMEM((rows, cols), jnp.float32),
            pltpu.SemaphoreType.DMA((2, GROUPS, 3)),
            pltpu.SemaphoreType.DMA((3,)),
        ],
    )(*[pltpu.with_memory_space_constraint(v, pltpu.HBM) for v in inputs])
    x_a, x_b = exchange(packed, packed, "bx")
    deep = lines + 2 * TILE
    send_a, send_b, corner = call(
        ends_kernel,
        [f32(deep, cols), f32(deep, cols), f32(TILE, cols)],
        "v" * 7,
    )(x_a, x_b, packed, top, bottom, weight, rhs)
    y_a, y_b = exchange(send_a, send_b, "by")
    size = ITERS + 1
    pairs = size * (size + 1) // 2
    rhs, strip, middle, sums = call(
        middle_kernel,
        [f32(rows, cols), f32(rows, cols), f32(size, rows - 2 * TILE, cols), f32(pairs, TILE, cols)],
        "v" * 6,
        cost=pl.CostEstimate(flops=200 * rows * cols, bytes_accessed=20 * rows * cols, transcendentals=0),
    )(x_a, x_b, packed, top, weight, rhs)
    outer, moments = call(
        rows_kernel,
        [f32(size, 2 * TILE, cols), f32(everyone, 1, cols)],
        "v" * 9,
    )(y_a, y_b, top, bottom, weight, rhs, strip, corner, sums)
    got = lax.all_to_all(moments, ("by", "bx"), 0, 0, tiled=True)
    new_tracers, = call(
        tracers_kernel,
        [f32(*tracers.shape)],
        "v" * 11,
        resident=False,
        cost=pl.CostEstimate(flops=30 * tracers.size, bytes_accessed=16 * tracers.size, transcendentals=0),
    )(tracers, velocity, diffusivity, kmt, packed, x_a, x_b, top, bottom, y_a, y_b)
    surface, residual, flag = call(
        solve_kernel,
        [f32(rows, cols), f32(rows, cols), jax.ShapeDtypeStruct((1, 1), jnp.int32)],
        "vvv",
        "hhs",
        scratch=[pltpu.VMEM((2, rows, cols), jnp.float32), pltpu.SemaphoreType.DMA((2,))],
    )(got, middle, outer)
    surface, residual = lax.cond(
        flag[0, 0] == 1,
        lambda: (surface, residual),
        lambda: step_by_step(jnp.concatenate([outer[0, :TILE], middle[0], outer[0, TILE:]]), inputs[3], inputs[5]),
    )
    return new_tracers, surface, residual


def solution(mesh):
    placed = (
        P(None, None, "by", "bx"),
        P(None, None, "by", "bx"),
        P(None, "by", "bx"),
        P("by", "bx"),
        P("by", "bx"),
        P("by", "bx"),
    )
    return jax.shard_map(
        per_device,
        mesh=mesh,
        in_specs=placed,
        out_specs=(P(None, None, "by", "bx"), P("by", "bx"), P("by", "bx")),
        check_vma=False,
    )
```

```python
import jax
import jax.numpy as jnp
from jax import lax
from jax.experimental import pallas as pl
from jax.experimental.pallas import tpu as pltpu
from jax.sharding import PartitionSpec as P


AXES = ("by", "bx")
ITERS = 4
TILE = 8
REACH = 4
CENTER = 5.0
HALFWIDTH = 4.0
VMEM_GRANT = 12 << 20
GROUPS = 2
LIMIT = 1000.0


def lanes_of(shape):
    return lax.broadcasted_iota(jnp.int32, shape, 1)


def rows_of(shape):
    return lax.broadcasted_iota(jnp.int32, shape, 0)


def roll(value, shift, axis=1):
    size = value.shape[axis]
    shift = shift % size
    return value if shift == 0 else pltpu.roll(value, shift, axis)


def tree_sum(values):
    while len(values) > 1:
        values = [sum(values[i : i + 2][1:], values[i]) for i in range(0, len(values), 2)]
    return values[0]


def unfold(block, rows, levels):
    half = block[: rows // 2]
    return jnp.concatenate([half, roll(half, -(6 * levels + 16))], axis=0)


def level_terms(kmt, k, di, u, v):
    wet = kmt > k
    mixing = jnp.where(wet, di, 0.0)
    across = jnp.where(wet, 0.5 * u, 0.0)
    along = jnp.where(wet, 0.5 * v, 0.0)
    return wet, 1.0 - 4.0 * mixing, mixing - across, mixing + across, mixing - along, mixing + along


def within(value, own, c_east, c_west, c_north, c_south):
    return (
        value * own
        + c_east * roll(value, -1)
        + c_west * roll(value, 1)
        + c_north * roll(value, -1, 0)
        + c_south * roll(value, 1, 0)
    )


def inside(c_east, c_west, c_north, c_south, lane, row):
    rows, cols = lane.shape
    return (
        jnp.where(lane == cols - 1, 0.0, c_east),
        jnp.where(lane == 0, 0.0, c_west),
        jnp.where(row == rows - 1, 0.0, c_north),
        jnp.where(row == 0, 0.0, c_south),
    )


def stencil_kernel(
    tr_hbm, ve_hbm, di_hbm, kmt_hbm, fo_hbm, fs_hbm, packed, top, bottom, rhs_out, weight, tr, ve, di, kmt_ref, fs, fo, sems, flat_sems
):
    levels = tr.shape[1]
    rows, cols = kmt_ref.shape
    chunk = rows // 2
    flat = [
        pltpu.make_async_copy(source, target, flat_sems.at[i])
        for i, (source, target) in enumerate(((kmt_hbm, kmt_ref), (fs_hbm, fs), (fo_hbm, fo)))
    ]
    for copy in flat:
        copy.start()
    span = levels // GROUPS
    copies = []
    for c, (begin, length) in enumerate(((0, chunk + TILE), (chunk + TILE, chunk - TILE))):
        part = pl.ds(begin, length)
        for g in range(GROUPS):
            deep = pl.ds(g * span, span)
            trio = (
                pltpu.make_async_copy(tr_hbm.at[:, deep, part], tr.at[:, deep, part], sems.at[c, g, 0]),
                pltpu.make_async_copy(ve_hbm.at[:, deep, part], ve.at[:, deep, part], sems.at[c, g, 1]),
                pltpu.make_async_copy(di_hbm.at[deep, part], di.at[deep, part], sems.at[c, g, 2]),
            )
            for copy in trio:
                copy.start()
            copies.append(trio)
    shape = (chunk, cols)
    lane, row = lanes_of(shape), rows_of(shape)
    base = 6 * levels
    first, last = lane == 0, lane == cols - 1
    lean = jnp.where(last, -0.5, 0.5)
    pack = jnp.zeros(shape, jnp.float32)
    for copy in flat:
        copy.wait()
    for c in range(rows // chunk):
        start = c * chunk
        part = pl.ds(start, chunk)
        kmt = kmt_ref[part, :]
        offset = c * (6 * levels + 16)
        heavy = jnp.where(kmt > 0, 4.0 + fs[part, :], 0.0)
        weight[part, :] = heavy
        mixed = jnp.zeros(shape, jnp.float32)
        carried = jnp.zeros(shape, jnp.float32)

        def row_jump(k, at):
            if at < 0 or at >= rows:
                return jnp.zeros((1, cols), jnp.float32)
            one = pl.ds(at, 1)
            return jnp.where(kmt_ref[one, :] > k, tr[0, k, one, :] - tr[1, k, one, :], 0.0)

        for k in range(levels):
            if k % span == 0:
                for copy in copies[c * GROUPS + k // span]:
                    copy.wait()
            wet = kmt > k
            values = [jnp.where(wet, tr[t, k, part, :], 0.0) for t in range(2)]
            mixing, u, v = di[k, part, :], ve[0, k, part, :], ve[1, k, part, :]
            edge = jnp.where(wet, mixing + lean * u, 0.0)
            for i, field in enumerate((*values, edge)):
                slot = offset // 2 + i * levels + k
                pack = jnp.where((lane // 2) == slot, roll(field, 2 * slot + 1), pack)
            jump = values[0] - values[1]
            east = jnp.where(last, 0.0, roll(jump, -1))
            west = jnp.where(first, 0.0, roll(jump, 1))
            north = jnp.where(row == chunk - 1, row_jump(k, start + chunk), roll(jump, -1, 0))
            south = jnp.where(row == 0, row_jump(k, start - 1), roll(jump, 1, 0))
            around = (east + west) + (north + south) - 4.0 * jump
            mixed = mixed + jnp.where(wet, jump + mixing * around, 0.0)
            carried = carried + jnp.where(wet, u * (east - west) + v * (north - south), 0.0)
            for ref, at, sign in ((bottom, 0, 0.5), (top, rows - 1, -0.5)):
                if start <= at < start + chunk:
                    here = slice(at - start, at - start + 1)
                    for i, field in enumerate(values):
                        ref[pl.ds(i * levels + k, 1), :] = field[here]
                    ref[pl.ds(2 * levels + k, 1), :] = jnp.where(wet[here], mixing[here] + sign * v[here], 0.0)
        rhs = jnp.where(kmt > 0, fo[part, :] + (mixed - 0.5 * carried) / levels, 0.0)
        rhs_out[part, :] = rhs
        for i, field in enumerate((rhs, heavy)):
            at = offset + base + 8 * i
            pack = jnp.where((lane // 8) == at // 8, roll(field, at + REACH), pack)
    packed[pl.ds(0, chunk), :] = pack
    small = (levels, cols)
    lane_s, row_s = lanes_of(small), rows_of(small)
    corner = jnp.zeros((TILE, cols), jnp.float32)
    row_c = rows_of((TILE, cols))
    for i, ref in enumerate((bottom, top)):
        jump = ref[pl.ds(0, levels), :] - ref[pl.ds(levels, levels), :]
        past = ref[pl.ds(2 * levels, levels), :]
        line = jnp.zeros(small, jnp.float32)
        for start, field in ((0, jump), (8 * levels, past)):
            spread = pltpu.roll(field, (start + REACH) % cols, 1, stride=8, stride_axis=0)
            line = line + jnp.where((lane_s // 8) == start // 8 + row_s, spread, 0.0)
        corner = jnp.where(row_c == i, jnp.sum(line, axis=0, keepdims=True), corner)
    packed[pl.ds(chunk, TILE), :] = corner


def tracers_kernel(tr, ve, di, kmt_ref, own_ref, east_west_a, east_west_b, top, bottom, north_south_a, north_south_b, new_out):
    levels = tr.shape[1]
    rows, cols = kmt_ref.shape
    shape = (rows, cols)
    lane, row = lanes_of(shape), rows_of(shape)
    kmt = kmt_ref[...]
    east, west = sides("bx", east_west_a[pl.ds(0, rows // 2), :], east_west_b[pl.ds(0, rows // 2), :])
    east, west = unfold(east, rows, levels), unfold(west, rows, levels)
    north, south = sides("by", north_south_a[pl.ds(0, 3 * levels), :], north_south_b[pl.ds(0, 3 * levels), :])
    beyond = jnp.where(lane % 2 == 0, roll(east, -1), roll(west, 1))
    mine = unfold(own_ref[pl.ds(0, rows // 2), :], rows, levels)
    ends = (lane == 0) | (lane == cols - 1)
    top_v, bottom_v = top[...], bottom[...]
    added = [mine * roll(beyond, 4 * levels - 2 * levels * t) for t in range(2)]
    above = [top_v[2 * levels :] * north[t * levels : (t + 1) * levels] for t in range(2)]
    below = [bottom_v[2 * levels :] * south[t * levels : (t + 1) * levels] for t in range(2)]
    for k in range(levels):
        wet, own, *around = level_terms(kmt, k, di[k], ve[0, k], ve[1, k])
        around = inside(*around, lane, row)
        for t in range(2):
            value = within(jnp.where(wet, tr[t, k], 0.0), own, *around)
            value = value + jnp.where(ends, roll(added[t], cols - 1 - (4 * levels + 2 * k)), 0.0)
            value = value + jnp.where(row == rows - 1, above[t][k : k + 1], 0.0) + jnp.where(row == 0, below[t][k : k + 1], 0.0)
            new_out[t, k] = value


def is_even(axis):
    return lax.axis_index(axis) % 2 == 0 if lax.axis_size(axis) % 2 == 0 else lax.axis_size(axis) > 0


def sides(axis, got_a, got_b):
    index, even = lax.axis_index(axis), is_even(axis)
    after = jnp.where(even, got_a, got_b)
    before = jnp.where(even, got_b, got_a)
    return jnp.where(index < lax.axis_size(axis) - 1, after, 0.0), jnp.where(index > 0, before, 0.0)


def complete(mine, e, w, rhs, levels, offset):
    cols = mine.shape[1]
    lane = lanes_of(mine.shape)
    even = lane % 2 == 0
    start = 4 * levels
    here = (lane >= start) & (lane < 6 * levels)
    ends = (lane == 0) | (lane == cols - 1)
    jump_mine = roll(mine, start - offset) - roll(mine, 2 * levels - offset)
    beyond = jnp.where(even, roll(e, -1 - offset), roll(w, 1 - offset))
    jump_e = roll(e, start - 1 - offset) - roll(e, 2 * levels - 1 - offset)
    jump_w = roll(w, start + 1 - offset) - roll(w, 2 * levels + 1 - offset)
    inward = jnp.where(here, roll(mine, -offset) * jnp.where(even, jump_e, jump_w), 0.0)
    outward = jnp.where(here, beyond * jump_mine, 0.0)
    added = tree_sum([roll(inward, cols - 1 - start - 2 * k) for k in range(levels)]) / levels
    passed = tree_sum([roll(outward, cols - 2 - start - 2 * k) for k in range(-1, levels)]) / levels
    strip = roll(jnp.where(lane % 8 < REACH, w, e), cols - REACH - 6 * levels - offset)
    return rhs + jnp.where(ends, added, 0.0), strip + jnp.where(ends, passed, 0.0)


def ends_kernel(got_a, got_b, packed, top, bottom, weight, rhs_in, send_a, send_b, corner_out):
    rows, cols = weight.shape
    levels = top.shape[0] // 3
    east, west = sides("bx", got_a[...], got_b[...])

    ends = []
    for first, begin, offset in ((0, 0, 0), (rows - TILE, rows // 2 - TILE, 6 * levels + 16)):
        part = slice(begin, begin + TILE)
        near = packed[pl.ds(begin, TILE), :]
        ends.append(complete(near, east[part], west[part], rhs_in[pl.ds(first, TILE), :], levels, offset))
    (rhs_low, strip_low), (rhs_high, strip_high) = ends
    tile = (TILE, cols)
    corner = jnp.where(lanes_of(tile) % 8 < REACH, west[rows // 2 :], east[rows // 2 :])
    corner_out[0] = corner
    corner_out[1] = roll(corner, 8 * levels)
    row = rows_of(tile)
    first, last = weight[pl.ds(0, TILE), :], weight[pl.ds(rows - TILE, TILE), :]
    n3 = 3 * levels
    above = (
        top[...],
        jnp.where(row < REACH, roll(last, REACH, 0), rhs_high),
        jnp.where(row == 0, corner[1:2], strip_high),
    )
    below = (
        bottom[...],
        jnp.where(row < REACH, rhs_low, roll(first, REACH, 0)),
        jnp.where(row == REACH, corner[:1], strip_low),
    )
    even = is_even("by")
    for ref, one, two in ((send_a, above, below), (send_b, below, above)):
        ref[pl.ds(0, n3), :] = jnp.where(even, one[0], two[0])
        ref[pl.ds(n3, TILE), :] = jnp.where(even, one[1], two[1])
        ref[pl.ds(n3 + TILE, TILE), :] = jnp.where(even, one[2], two[2])


def krylov(rhs_c, heavy_c, strip):
    lane = lanes_of(rhs_c.shape)
    cols = rhs_c.shape[1]
    near = (lane < REACH) | (lane >= cols - REACH)
    rhs_s, heavy_s = jnp.where(near, strip, 0.0), jnp.where(near, roll(strip, -8), 0.0)
    scale = 1.0 / HALFWIDTH
    diag_c, side_c = jnp.where(heavy_c > 0, (heavy_c - CENTER) * scale, 0.0), jnp.where(heavy_c > 0, scale, 0.0)
    diag_s, side_s = jnp.where(heavy_s > 0, (heavy_s - CENTER) * scale, 0.0), jnp.where(heavy_s > 0, scale, 0.0)
    right, left = lane == cols - 1, lane == 0

    def apply(c, s):
        rc, rs, lc, ls = roll(c, -1), roll(s, -1), roll(c, 1), roll(s, 1)
        around_c = jnp.where(right, rs, rc) + jnp.where(left, ls, lc) + roll(c, -1, 0) + roll(c, 1, 0)
        around_s = jnp.where(right, rc, rs) + jnp.where(left, lc, ls) + roll(s, -1, 0) + roll(s, 1, 0)
        return diag_c * c - side_c * around_c, diag_s * s - side_s * around_s

    vectors = [(rhs_c, rhs_s)]
    vectors.append(apply(*vectors[0]))
    for _ in range(ITERS - 1):
        c, s = apply(*vectors[-1])
        vectors.append((2.0 * c - vectors[-2][0], 2.0 * s - vectors[-2][1]))
    return [c for c, _ in vectors]


def products(vectors):
    cols = vectors[0].shape[1]
    return [
        (vectors[i] * vectors[j]).reshape(-1, TILE, cols).sum(axis=0)
        for i in range(len(vectors))
        for j in range(i, len(vectors))
    ]


def middle_kernel(got_a, got_b, packed, top, weight, rhs_in, rhs_out, strip_out, basis, sums):
    rows, _ = weight.shape
    levels = top.shape[0] // 3
    east, west = sides("bx", got_a[pl.ds(0, rows // 2), :], got_b[pl.ds(0, rows // 2), :])
    mine = packed[pl.ds(0, rows // 2), :]
    half = rows // 2
    parts = [
        complete(mine, east, west, rhs_in[pl.ds(i * half, half), :], levels, i * (6 * levels + 16)) for i in range(2)
    ]
    rhs, strip = (jnp.concatenate(pair, axis=0) for pair in zip(*parts))
    rhs_out[...] = rhs
    strip_out[...] = strip
    vectors = [v[TILE : rows - TILE] for v in krylov(rhs, weight[...], strip)]
    for i, v in enumerate(vectors):
        basis[i] = v
    for i, v in enumerate(products(vectors)):
        sums[i] = v


def rows_kernel(got_a, got_b, top, bottom, weight, rhs_in, strip_in, corner_in, sums, basis, moments):
    rows, cols = weight.shape
    levels = top.shape[0] // 3
    north, south = sides("by", got_a[...], got_b[...])
    n3 = 3 * levels

    def jump(block):
        return block[:levels] - block[levels : 2 * levels]

    def dot(coefficient, value):
        return jnp.sum(coefficient * value, axis=0, keepdims=True) / levels

    top_v, bottom_v = top[...], bottom[...]
    add_top = dot(top_v[2 * levels :], jump(north[:n3]))
    add_bottom = dot(bottom_v[2 * levels :], jump(south[:n3]))
    add_north = dot(north[2 * levels : n3], jump(top_v))
    add_south = dot(south[2 * levels : n3], jump(bottom_v))
    turned = corner_in[1]
    c_north, c_south = north[n3 + TILE + REACH : n3 + TILE + REACH + 1], south[n3 + TILE : n3 + TILE + 1]
    edge = (1, cols)
    lane_1 = lanes_of(edge)
    tile = (TILE, cols)
    crossed = jnp.where(rows_of(tile) == 0, c_north * turned[1:2], c_south * turned[:1])
    lower = lanes_of(tile) < 8 * levels
    near = (lanes_of(tile) < REACH) | (lanes_of(tile) >= cols - REACH)
    gain, given = jnp.where(lower, crossed, 0.0), jnp.where(lower, 0.0, crossed)
    gain = tree_sum([roll(gain, cols - REACH - 8 * k) for k in range(levels)]) / levels
    given = tree_sum([roll(given, cols - REACH - 8 * levels - 8 * k) for k in range(levels)]) / levels
    gain, given = jnp.where(near, gain, 0.0), jnp.where(near, given, 0.0)
    strip_top, strip_bottom, strip_north, strip_south = gain[:1], gain[1:2], given[:1], given[1:2]
    outer = rows_of((TILE, cols))
    flat_n, flat_s = north[n3 : n3 + TILE], south[n3 : n3 + TILE]

    def bands(ref, below, above):
        pieces = [jnp.where(outer >= TILE - REACH, below, 0.0), ref[pl.ds(0, 2 * TILE), :]]
        pieces += [ref[pl.ds(rows - 2 * TILE, 2 * TILE), :], jnp.where(outer < REACH, above, 0.0)]
        return jnp.concatenate(pieces, axis=0)

    row = rows_of((6 * TILE, cols))

    def patch(field, at_south, at_bottom, at_top, at_north):
        field = field + jnp.where(row == TILE - 1, at_south, 0.0) + jnp.where(row == TILE, at_bottom, 0.0)
        return field + jnp.where(row == 5 * TILE - 1, at_top, 0.0) + jnp.where(row == 5 * TILE, at_north, 0.0)

    rhs_c = patch(bands(rhs_in, flat_s, flat_n), add_south, add_bottom, add_top, add_north)
    heavy_c = bands(weight, roll(flat_s, REACH, 0), roll(flat_n, REACH, 0))
    strip = bands(strip_in, south[n3 + TILE :], north[n3 + TILE :])
    strip = patch(strip, strip_south, strip_bottom, strip_top, strip_north)
    vectors = krylov(rhs_c, heavy_c, strip)
    vectors = [jnp.concatenate([v[TILE : 2 * TILE], v[4 * TILE : 5 * TILE]], axis=0) for v in vectors]
    line = jnp.zeros(edge, jnp.float32)
    for i, v in enumerate(vectors):
        basis[i] = v
    for i, v in enumerate(products(vectors)):
        whole = jnp.sum(jnp.sum(v + sums[i], axis=0, keepdims=True), axis=1, keepdims=True)
        line = jnp.where(lane_1 == i, whole, line)
    moments[...] = jnp.broadcast_to(line[None], moments.shape)


def times(coefficients):
    out = [None] * (len(coefficients) + 1)

    def put(at, value):
        out[at] = value if out[at] is None else out[at] + value

    for j, c in enumerate(coefficients):
        put(j, CENTER * c)
        if j == 0:
            put(1, HALFWIDTH * c)
        else:
            put(j + 1, 0.5 * HALFWIDTH * c)
            put(j - 1, 0.5 * HALFWIDTH * c)
    return out


def mix(a, b, factor):
    out = []
    for j in range(max(len(a), len(b))):
        if j >= len(b):
            out.append(a[j])
        elif j >= len(a):
            out.append(factor * b[j])
        else:
            out.append(a[j] + factor * b[j])
    return out


def solve_kernel(got, middle, outer, surface_out, residual_out, flag, results, sems):
    size = ITERS + 1
    line = jnp.sum(got[...], axis=0)
    lane_1 = lanes_of(line.shape)
    gram, at = {}, 0
    for i in range(size):
        for j in range(i, size):
            gram[i, j] = gram[j, i] = jnp.sum(jnp.where(lane_1 == at, line, 0.0), axis=1, keepdims=True)
            at += 1

    def inner(a, b):
        exact = bound = None
        for i, x in enumerate(a):
            for j, y in enumerate(b):
                term = x * y * gram[i, j]
                exact = term if exact is None else exact + term
                bound = jnp.abs(term) if bound is None else bound + jnp.abs(term)
        return exact, bound

    one = jnp.ones_like(gram[0, 0])
    good = one > 0
    residual = [one]
    image = times(residual)
    now, _ = inner(residual, residual)
    product, _ = inner(residual, image)
    alpha = now / product
    direction, along = residual, image
    surface = []
    for step in range(ITERS):
        surface = mix(surface, direction, alpha)
        residual = mix(residual, along, -alpha)
        if step + 1 < ITERS:
            image = times(residual)
            following, bound = inner(residual, residual)
            good = good & (bound <= LIMIT * following)
            product, bound = inner(residual, image)
            good = good & (bound <= LIMIT * product)
            ratio = following / now
            taken = ratio * following / alpha
            good = good & (product + taken <= 0.1 * LIMIT * (product - taken))
            alpha = following / (product - taken)
            direction = mix(residual, direction, ratio)
            along = mix(image, along, ratio)
            now = following
    last, _ = inner(residual, residual)
    good = good & (now <= 0.1 * LIMIT * last)
    rows = surface_out.shape[0]
    copies = []
    for at, (ref, combination) in enumerate(((surface_out, surface), (residual_out, residual))):
        for part, first, last in ((middle, TILE, rows - TILE), (outer, 0, 2 * TILE)):
            total = combination[0] * part[0]
            for j in range(1, len(combination)):
                total = total + combination[j] * part[j]
            if part is middle:
                results[at, pl.ds(first, last - first), :] = total
            else:
                results[at, pl.ds(0, TILE), :] = total[:TILE]
                results[at, pl.ds(rows - TILE, TILE), :] = total[TILE:]
        copies.append(pltpu.make_async_copy(results.at[at], ref, sems.at[at]))
        copies[at].start()
    flag[0, 0] = jnp.where(good, 1, 0)[0, 0]
    for copy in copies:
        copy.wait()


def linear(axis, index, other):
    row, column = (index, other) if axis == AXES[0] else (other, index)
    return row * lax.axis_size(AXES[1]) + column


def exchange(first, second, axis):
    peers = lax.axis_size(axis)
    if peers % 2:
        up = [(i, i + 1) for i in range(peers - 1)]
        down = [(j, i) for i, j in up]
        return lax.ppermute(second, axis, down), lax.ppermute(first, axis, up)
    pairs_a = [(i, i ^ 1) for i in range(peers)]
    pairs_b = [(i, (i + 1) % peers if i % 2 else (i - 1) % peers) for i in range(peers)]
    other, = [name for name in AXES if name != axis]
    if lax.axis_size(other) % 2 == 0:
        far = []
        for i in range(peers):
            for j in range(lax.axis_size(other)):
                target = (i, j ^ 1) if i in (0, peers - 1) else (pairs_b[i][1], j)
                far.append((linear(axis, i, j), linear(axis, *target)))
        axes, pairs_b = AXES, far
    else:
        axes = axis
    got_a = lax.ppermute(first, axis, pairs_a)
    got_b = lax.ppermute(second, axes, pairs_b)
    return got_a, got_b


def padded_2(value, axes, width):
    for axis, dim in axes:
        peers, length = (lax.axis_size(axis), value.shape[dim])
        up = [(i, (i + 1) % peers) for i in range(peers - 1)]
        down = [(j, i) for i, j in up]
        last = lax.slice_in_dim(value, length - width, length, axis=dim)
        first = lax.slice_in_dim(value, 0, width, axis=dim)
        before = lax.ppermute(last, axis, up)
        after = lax.ppermute(first, axis, down)
        value = jnp.concatenate([before, value, after], axis=dim)
    return value


def step_by_step(rhs, kmt, free_surface):
    ocean = (kmt > 0).astype(jnp.float32)
    weight = ocean * (4.0 + free_surface)

    def operate(field):
        padded = padded_2(field, (("by", 0), ("bx", 1)), 1)
        around = padded[1:-1, 2:] + padded[1:-1, :-2] + padded[2:, 1:-1] + padded[:-2, 1:-1]
        return weight * field - ocean * around

    def pair(a, b):
        return lax.psum(lax.psum((jnp.sum(a * a), jnp.sum(a * b)), "bx"), "by")

    surface, residual = jnp.zeros_like(rhs), rhs
    image = operate(residual)
    now, product = pair(residual, image)
    alpha = now / product
    direction, along = residual, image
    for step in range(ITERS):
        surface = surface + alpha * direction
        residual = residual - alpha * along
        if step + 1 < ITERS:
            image = operate(residual)
            following, product = pair(residual, image)
            ratio = following / now
            alpha = following / (product - ratio * following / alpha)
            direction = residual + ratio * direction
            along = image + ratio * along
            now = following
    return surface, residual


def call(kernel, out_shape, kinds, out_kinds=None, scratch=(), cost=None, resident=True):
    spaces = {"s": pltpu.SMEM, "v": pltpu.VMEM, "h": pltpu.HBM}
    out_kinds = out_kinds or "v" * len(out_shape)
    if resident:
        out_shape = [spaces[k](o.shape, o.dtype) for k, o in zip(out_kinds, out_shape)]
    return pl.pallas_call(
        kernel,
        out_shape=out_shape,
        in_specs=[pl.BlockSpec(memory_space=spaces[k]) for k in kinds],
        out_specs=[pl.BlockSpec(memory_space=spaces[k]) for k in out_kinds],
        scratch_shapes=scratch,
        cost_estimate=cost,
        compiler_params=pltpu.CompilerParams(vmem_limit_bytes=VMEM_GRANT),
    )


def f32(*shape):
    return jax.ShapeDtypeStruct(shape, jnp.float32)


def per_device(*inputs):
    tracers, kmt = inputs[0], inputs[3]
    levels = tracers.shape[1]
    rows, cols = kmt.shape
    everyone = lax.axis_size("by") * lax.axis_size("bx")
    lines = 3 * levels
    packed, top, bottom, rhs, weight, tracers, velocity, diffusivity, kmt = call(
        stencil_kernel,
        [f32(rows // 2 + TILE, cols), f32(lines, cols), f32(lines, cols), f32(rows, cols), f32(rows, cols)]
        + [jax.ShapeDtypeStruct(v.shape, v.dtype) for v in inputs[:4]],
        "h" * 6,
        scratch=[
            pltpu.VMEM((rows, cols), jnp.float32),
            pltpu.VMEM((rows, cols), jnp.float32),
            pltpu.SemaphoreType.DMA((2, GROUPS, 3)),
            pltpu.SemaphoreType.DMA((3,)),
        ],
    )(*[pltpu.with_memory_space_constraint(v, pltpu.HBM) for v in inputs])
    x_a, x_b = exchange(packed, packed, "bx")
    deep = lines + 2 * TILE
    send_a, send_b, corner = call(
        ends_kernel,
        [f32(deep, cols), f32(deep, cols), f32(2, TILE, cols)],
        "v" * 7,
    )(x_a, x_b, packed, top, bottom, weight, rhs)
    y_a, y_b = exchange(send_a, send_b, "by")
    size = ITERS + 1
    pairs = size * (size + 1) // 2
    rhs, strip, middle, sums = call(
        middle_kernel,
        [f32(rows, cols), f32(rows, cols), f32(size, rows - 2 * TILE, cols), f32(pairs, TILE, cols)],
        "v" * 6,
        cost=pl.CostEstimate(flops=200 * rows * cols, bytes_accessed=20 * rows * cols, transcendentals=0),
    )(x_a, x_b, packed, top, weight, rhs)
    outer, moments = call(
        rows_kernel,
        [f32(size, 2 * TILE, cols), f32(everyone, 1, cols)],
        "v" * 9,
    )(y_a, y_b, top, bottom, weight, rhs, strip, corner, sums)
    got = lax.all_to_all(moments, ("by", "bx"), 0, 0, tiled=True)
    new_tracers, = call(
        tracers_kernel,
        [f32(*tracers.shape)],
        "v" * 11,
        resident=False,
        cost=pl.CostEstimate(flops=30 * tracers.size, bytes_accessed=16 * tracers.size, transcendentals=0),
    )(tracers, velocity, diffusivity, kmt, packed, x_a, x_b, top, bottom, y_a, y_b)
    surface, residual, flag = call(
        solve_kernel,
        [f32(rows, cols), f32(rows, cols), jax.ShapeDtypeStruct((1, 1), jnp.int32)],
        "vvv",
        "hhs",
        scratch=[pltpu.VMEM((2, rows, cols), jnp.float32), pltpu.SemaphoreType.DMA((2,))],
    )(got, middle, outer)
    surface, residual = lax.cond(
        flag[0, 0] == 1,
        lambda: (surface, residual),
        lambda: step_by_step(jnp.concatenate([outer[0, :TILE], middle[0], outer[0, TILE:]]), inputs[3], inputs[5]),
    )
    return new_tracers, surface, residual


def solution(mesh):
    placed = (
        P(None, None, "by", "bx"),
        P(None, None, "by", "bx"),
        P(None, "by", "bx"),
        P("by", "bx"),
        P("by", "bx"),
        P("by", "bx"),
    )
    return jax.shard_map(
        per_device,
        mesh=mesh,
        in_specs=placed,
        out_specs=(P(None, None, "by", "bx"), P("by", "bx"), P("by", "bx")),
        check_vma=False,
    )
```
